32 devices in a mesh: aux: 8 (over z, core), grp: 4 (over y, x).
Axes of the slice: x: 2, y: 2, z: 4, core: 2. Of those that a mesh axis runs over, the one named last changes fastest.
Arguments:
- integrals: bfloat16 [1024, 512, 256], P('aux', 'grp'), may hold values from -2.5 to 2.5
- metric: bfloat16 [1024, 1024], replicated, may hold values from -0.1875 to 0.1875
- fock: bfloat16 [512, 512], replicated, may hold values from -2 to 0.5, as said below
- virt_energy: float32 [256], replicated, may hold values from 0.3 to 3
- send_orb: int32 [32, 4], P(('aux', 'grp')), may hold values from 0 to 15, as said below
- pair_orb: int32 [512, 2], P(('aux', 'grp')), may hold values from 0 to 511, as said below
- send_pair: int32 [32, 4], P(('aux', 'grp')), may hold values from 0 to 15, as said below
- cpl_slot: int32 [512, 4], P(('aux', 'grp')), may hold values from 0 to 3, as said below
- cpl_orb: int32 [512, 4, 2], P(('aux', 'grp')), may hold values from 0 to 511, as said below
Outputs:
- amplitudes: float32 [512, 256, 256], P(('aux', 'grp'))
The draws below stay inside these ranges and needn't reach their ends.
Inputs may be any that keep to these rules, and one draw needn't show every extreme that they name: send_orb is below 16. `pair_orb`: the orbitals of the pairs owned by device (col, g) lie in column col: an orbital o of them has (o % 128) // 16 == col and o % 16 == send_orb[col * 4 + o // 128, g]. No pair is listed twice on a device. send_pair indexes the sending device's own pairs. `cpl_slot`: the entries of one pair are distinct. cpl_orb[p, e] equals pair_orb of the pair q[p, e] defined in the reference program. fock is symmetric with diagonal entries between -2 and -0.5.
All inputs are finite; a program needn't handle non-finite values.
Results may differ from the reference program's by a relative error of at most 0.0027.
Values may be sent and summed in bfloat16 or wider, within the bound.
A program may use at most 128 MiB of HBM per device.

```python
import math
import jax
import jax.numpy as jnp
from jax import lax

NAUX = 1024
NOCC = 512
NV = 256
PAIRS = 16
NC = 4
ITERS = 2
N_AUX = 8
N_GRP = 4


def routing(key):
    base = jax.random.fold_in(key, 9173)
    keys = jax.random.split(base, 4)
    ndev = N_AUX * N_GRP
    orb_dev = NOCC // ndev
    group_orbs = NOCC // N_GRP
    grid = N_GRP * N_GRP
    send_orb = jax.random.randint(keys[0], (N_AUX, N_GRP, N_GRP), 0, orb_dev).astype(jnp.int32)
    col_base = jnp.arange(N_AUX, dtype=jnp.int32)[:, None, None] * orb_dev
    grp_base = jnp.arange(N_GRP, dtype=jnp.int32)[None, :, None] * group_orbs
    slot_orb = grp_base + col_base + send_orb
    received = jnp.transpose(slot_orb, (0, 2, 1))
    noise = jax.random.randint(keys[1], (N_AUX, N_GRP, grid), 0, 1 << 20)
    order = jnp.argsort(noise * grid + jnp.arange(grid, dtype=jnp.int32), axis=-1)[:, :, :PAIRS]
    orb_first = jnp.take_along_axis(received, order // N_GRP, axis=2)
    orb_second = jnp.take_along_axis(received, order % N_GRP, axis=2)
    left_i = orb_first[:, :, :, None, None]
    left_j = orb_second[:, :, :, None, None]
    right_k = orb_first[:, None, None, :, :]
    right_l = orb_second[:, None, None, :, :]
    share = (right_l == left_j) & (right_k != left_i) | (right_k == left_i) & (right_l != left_j)
    count = jnp.sum(share.astype(jnp.int32), axis=2)
    tie = jax.random.randint(keys[2], (N_AUX, N_GRP, N_GRP, PAIRS), 0, 1 << 10)
    score = count * (1 << 20) + tie * PAIRS + jnp.arange(PAIRS, dtype=jnp.int32)
    best = jnp.argmax(score, axis=-1).astype(jnp.int32)
    send_pair = jnp.transpose(best, (0, 2, 1))
    pick = best[..., None] == jnp.arange(PAIRS, dtype=jnp.int32)
    sent_first = jnp.sum(jnp.where(pick, orb_first[:, None, :, :], 0), axis=-1)
    sent_second = jnp.sum(jnp.where(pick, orb_second[:, None, :, :], 0), axis=-1)
    own_i = orb_first[..., None]
    own_j = orb_second[..., None]
    got_k = sent_first[:, :, None, :]
    got_l = sent_second[:, :, None, :]
    share_two = (got_l == own_j) & (got_k != own_i) | (got_k == own_i) & (got_l != own_j)
    tie_two = jax.random.randint(keys[3], (N_AUX, N_GRP, PAIRS, N_GRP), 0, 1 << 10)
    score_two = share_two.astype(jnp.int32) * (1 << 20) + tie_two * N_GRP + jnp.arange(N_GRP, dtype=jnp.int32)
    unused, chosen = lax.top_k(score_two, NC)
    chosen = chosen.astype(jnp.int32)
    shape_full = (N_AUX, N_GRP, PAIRS, N_GRP)
    cpl_first = jnp.take_along_axis(jnp.broadcast_to(got_k, shape_full), chosen, axis=3)
    cpl_second = jnp.take_along_axis(jnp.broadcast_to(got_l, shape_full), chosen, axis=3)
    pair_orb = jnp.stack([orb_first, orb_second], axis=-1).reshape(ndev * PAIRS, 2)
    cpl_orb = jnp.stack([cpl_first, cpl_second], axis=-1).reshape(ndev * PAIRS, NC, 2)
    return (send_orb.reshape(ndev, N_GRP).astype(jnp.int32), pair_orb.astype(jnp.int32), send_pair.reshape(ndev, N_GRP).astype(jnp.int32), chosen.reshape(ndev * PAIRS, NC), cpl_orb.astype(jnp.int32))


def draw_send_orb(key, part):
    return routing(key)[0]


def draw_pair_orb(key, part):
    return routing(key)[1]


def draw_send_pair(key, part):
    return routing(key)[2]


def draw_cpl_slot(key, part):
    return routing(key)[3]


def draw_cpl_orb(key, part):
    return routing(key)[4]


def draw_fock(key, part):
    base = jax.random.fold_in(key, 311)
    key_off, key_diag = jax.random.split(base)
    raw = jnp.clip(jax.random.normal(key_off, (NOCC, NOCC), jnp.float32), -4.0, 4.0) * 0.15
    symmetric = jnp.clip((raw + raw.T) * 0.7071, -0.5, 0.5)
    diag = -jax.random.uniform(key_diag, (NOCC,), jnp.float32, 0.5, 2.0)
    eye = jnp.eye(NOCC, dtype=jnp.float32)
    return (symmetric * (1.0 - eye) + eye * diag[None, :]).astype(jnp.bfloat16)


def steps_of(key, extent, cuts, smallest, largest):
    level, own = 1.0, jax.random.fold_in(key, 6)
    for position, blocks in cuts:
        steps = jnp.exp(jax.random.uniform(jax.random.fold_in(own, position), (blocks,), jnp.float32, smallest / len(cuts), largest / len(cuts)))
        level = level * jnp.repeat(steps, extent[position] // blocks).reshape([-1 if axis == position else 1 for axis in range(len(extent))])
    return level


def bell_draw(rng, dims, width, bound, cuts=(), held_as=jnp.bfloat16):
    factor_of = steps_of(rng, dims, cuts, -0.22, 0.18) if cuts else 1.0
    result = jax.random.normal(rng, dims, jnp.float32) * width * factor_of
    return jnp.minimum(jnp.maximum(result, -bound), bound).astype(held_as)


def setup_inputs(seed: int = 0) -> dict:
    seeds = jax.random.split(jax.random.key(seed), 10)
    integrals = bell_draw(seeds[0], (NAUX, NOCC, NV), (NAUX ** -0.25), 2.5, ((0, 8), (1, 4)))
    metric = bell_draw(seeds[1], (NAUX, NAUX), NAUX ** -0.5, 0.1875)
    fock = draw_fock(jax.random.fold_in(seeds[9], 71), 0)
    virt_energy = jnp.clip(jnp.exp(jax.random.uniform(seeds[3], (NV,), jnp.float32, math.log(0.3), math.log(3.0))), 0.3, 3.0)
    send_orb = draw_send_orb(jax.random.fold_in(seeds[9], 71), 0)
    pair_orb = draw_pair_orb(jax.random.fold_in(seeds[9], 71), 0)
    send_pair = draw_send_pair(jax.random.fold_in(seeds[9], 71), 0)
    cpl_slot = draw_cpl_slot(jax.random.fold_in(seeds[9], 71), 0)
    cpl_orb = draw_cpl_orb(jax.random.fold_in(seeds[9], 71), 0)
    return {"integrals": integrals, "metric": metric, "fock": fock, "virt_energy": virt_energy, "send_orb": send_orb, "pair_orb": pair_orb, "send_pair": send_pair, "cpl_slot": cpl_slot, "cpl_orb": cpl_orb}


def fitted_all(integrals, metric):
    flat = integrals.reshape(NAUX, NOCC * NV)
    fitted = jnp.dot(metric, flat, preferred_element_type=jnp.float32)
    return fitted.astype(jnp.bfloat16).reshape(NAUX, NOCC, NV)


def reference(integrals, metric, fock, virt_energy, send_orb, pair_orb, send_pair, cpl_slot, cpl_orb):
    fock = fock.astype(jnp.float32)
    ndev = N_AUX * N_GRP
    group_orbs = NOCC // N_GRP
    orb_dev = NOCC // ndev
    fitted = fitted_all(integrals, metric)
    device = (jnp.arange(ndev * PAIRS, dtype=jnp.int32) // PAIRS).astype(jnp.int32)
    column = device // N_GRP
    group = device % N_GRP

    def routed(orbital):
        source = orbital // group_orbs
        chosen = send_orb[column * N_GRP + source, group]
        return (source * group_orbs + column * orb_dev + chosen).astype(jnp.int32)

    orb_i = pair_orb[:, 0]
    orb_j = pair_orb[:, 1]
    src_i = routed(orb_i).reshape(ndev, PAIRS)
    src_j = routed(orb_j).reshape(ndev, PAIRS)

    def pair_block(args):
        left_idx, right_idx = args
        left = jnp.take(fitted, left_idx, axis=1).astype(jnp.float32)
        right = jnp.take(fitted, right_idx, axis=1).astype(jnp.float32)
        return jnp.einsum("qpa,qpb->pab", left, right)

    kmat = lax.map(pair_block, (src_i, src_j))
    diag_sum = (fock[orb_i, orb_i] + fock[orb_j, orb_j]).reshape(ndev, PAIRS)

    k_orb = cpl_orb[:, :, 0]
    l_orb = cpl_orb[:, :, 1]
    first = (l_orb == orb_j[:, None]) & (k_orb != orb_i[:, None])
    second = (k_orb == orb_i[:, None]) & (l_orb != orb_j[:, None])
    f_ik = fock[orb_i[:, None], k_orb]
    f_jl = fock[orb_j[:, None], l_orb]
    weight = (jnp.where(first, f_ik, jnp.float32(0.0)) + jnp.where(second, f_jl, jnp.float32(0.0))).reshape(ndev, PAIRS, NC)

    dev_ids = jnp.arange(ndev, dtype=jnp.int32)
    dev_col = dev_ids // N_GRP
    dev_grp = dev_ids % N_GRP
    sender = (dev_col[:, None] * N_GRP + jnp.arange(N_GRP, dtype=jnp.int32)[None, :]).astype(jnp.int32)
    qtab = (sender * PAIRS + send_pair[sender, dev_grp[:, None]]).astype(jnp.int32)
    slots = cpl_slot.reshape(ndev, PAIRS, NC)
    qpair = jnp.take_along_axis(jnp.broadcast_to(qtab[:, None, :], (ndev, PAIRS, N_GRP)), slots, axis=2)

    def denominator(dsum):
        return (virt_energy[:, None] + virt_energy[None, :])[None, :, :] - dsum[:, None, None]

    def start(args):
        kblk, dsum = args
        return -(kblk / denominator(dsum))

    amps = lax.map(start, (kmat, diag_sum))
    for step in range(ITERS):
        rounded = amps.astype(jnp.bfloat16).reshape(ndev * PAIRS, NV, NV)

        def update(args):
            kblk, ablk, dsum, wblk, qrow = args
            den = denominator(dsum)
            coupled = jnp.take(rounded, qrow.reshape(-1), axis=0).astype(jnp.float32).reshape(PAIRS, NC, NV, NV)
            term = jnp.einsum("pc,pcab->pab", wblk, coupled)
            resid = kblk + den * ablk - term
            return ablk - resid / den

        amps = lax.map(update, (kmat, amps, diag_sum, weight, qpair))
    return amps.reshape(ndev * PAIRS, NV, NV)
```

```python
import functools

import jax
import jax.numpy as jnp
from jax import lax
from jax.experimental import pallas as pl
from jax.experimental.pallas import tpu as pltpu
from jax.sharding import PartitionSpec as P

ITERS = 2
MESH = pl.DeviceIdType.MESH
F32 = jnp.float32
BF16 = jnp.bfloat16
NT = (((1,), (1,)), ((), ()))
LANES = 128


def chunks_of(nv):
    cuts = [0, nv // 2, nv * 3 // 4, nv * 7 // 8, nv]
    return list(zip(cuts[:-1], cuts[1:]))


def up(n):
    return -(-n // LANES) * LANES


def fused_kernel(
    dims,
    integrals, metric, fock, ve_row, send_orb, pair_s, pair_v, send_pair, slot_v, cpl_v,
    out,
    raw, pk, it, ft, met, fk, vsum, idx_tx, idx_rx, wt_v, wt_s,
    gs, tx, rx,
    raw_sem, met_sem, fk_sem, wt_sem, idx_send, idx_recv, own_sem,
    a_send, a_recv, x_send, x_recv,
):
    n_aux, n_grp, rows, od, nv, pairs, group_orbs, chunks = dims
    a = lax.axis_index("aux")
    g = lax.axis_index("grp")
    n_dev = n_aux * n_grp
    half = n_aux // 2

    def col_of(k):
        off = half + jnp.where(k % 2 == 0, k // 2, -((k + 1) // 2))
        return lax.rem(a + off, n_aux)

    def raw_copy(k, col):
        first = pl.multiple_of(col * od, od)
        return pltpu.make_async_copy(integrals.at[:, pl.ds(first, od), :], raw.at[k], raw_sem.at[k])

    barrier = pltpu.get_barrier_semaphore()

    @pl.loop(1, n_dev)
    def _(k):
        t = lax.rem(a * n_grp + g + k, n_dev)
        pl.semaphore_signal(barrier, inc=1, device_id=(t // n_grp, t % n_grp), device_id_type=MESH)

    @pl.loop(0, n_aux)
    def _(k):
        raw_copy(k, col_of(k)).start()

    met_copy = pltpu.make_async_copy(metric, met, met_sem)
    fk_copy = pltpu.make_async_copy(fock, fk, fk_sem)
    met_copy.start()
    fk_copy.start()
    for s in range(n_grp):
        idx_tx[pl.ds(s, 1), :] = jnp.full((1, LANES), send_orb[0, s], jnp.int32)
        idx_rx[a, pl.ds(s, 1), :] = jnp.full((1, LANES), send_orb[0, s], jnp.int32)

    pl.semaphore_wait(barrier, n_dev - 1)

    def idx_copy(k):
        t = lax.rem(a + k, n_aux)
        return pltpu.make_async_remote_copy(
            src_ref=idx_tx, dst_ref=idx_rx.at[a], send_sem=idx_send, recv_sem=idx_recv,
            device_id=(t, g), device_id_type=MESH,
        )

    @pl.loop(1, n_aux)
    def _(k):
        idx_copy(k).start()

    idx_all = pltpu.make_async_copy(idx_rx.at[pl.ds(1, n_aux - 1)], idx_rx.at[pl.ds(1, n_aux - 1)], idx_recv)
    idx_all.wait()

    def block_copy(c, col, grp):
        c0, c1 = chunks[c]
        lane0 = pl.multiple_of(a * rows, rows)
        return pltpu.make_async_remote_copy(
            src_ref=pk.at[col * n_grp + grp, pl.ds(c0, c1 - c0), :],
            dst_ref=it.at[g, pl.ds(c0, c1 - c0), pl.ds(lane0, rows)],
            send_sem=a_send.at[c], recv_sem=a_recv.at[c],
            device_id=(col, grp), device_id_type=MESH,
        )

    def own_copy(c):
        c0, c1 = chunks[c]
        lane0 = pl.multiple_of(a * rows, rows)
        return pltpu.make_async_copy(
            pk.at[a * n_grp + g, pl.ds(c0, c1 - c0), :],
            it.at[g, pl.ds(c0, c1 - c0), pl.ds(lane0, rows)],
            own_sem.at[c],
        )

    def send_far(c, k):
        col = col_of(k)
        for d in range(n_grp):
            block_copy(c, col, lax.rem(g + d, n_grp)).start()

    def send_own(c):
        for d in range(1, n_grp):
            block_copy(c, a, lax.rem(g + d, n_grp)).start()
        own_copy(c).start()

    step = 2 * LANES // od
    lane = lax.broadcasted_iota(jnp.int32, (step, 2 * LANES), 1)
    row = lax.broadcasted_iota(jnp.int32, (step, 2 * LANES), 0)

    def select(k, col):
        raw_copy(k, col).wait()
        pick = []
        for s in range(n_grp):
            v = idx_rx[col, pl.ds(s, 1), :]
            v = jnp.broadcast_to(jnp.concatenate([v, v], axis=1), (step, 2 * LANES))
            pick.append(jnp.where(lane == row * od + v, 1.0, 0.0))
        sel = jnp.concatenate(pick, axis=0).astype(BF16)
        parts = []
        for t in range(rows // step):
            x = raw[k, t * step:(t + 1) * step].reshape(step * od, nv)
            parts.append(jnp.dot(sel, x, preferred_element_type=F32))
        for s in range(n_grp):
            blk = jnp.concatenate([p[s * step:(s + 1) * step] for p in parts], axis=0)
            pk[col * n_grp + s] = jnp.transpose(blk).astype(BF16)

    @pl.loop(0, n_aux - 1)
    def _(k):
        select(k, col_of(k))
        send_far(0, k)

    select(n_aux - 1, a)
    send_own(0)

    def send_chunk(c):
        @pl.loop(0, n_aux - 1)
        def _(k):
            send_far(c, k)

        send_own(c)

    send_chunk(1)

    ve = ve_row[...]
    vb = jnp.broadcast_to(ve, (nv, nv))
    vsum[...] = jnp.transpose(vb) + vb

    fk_copy.wait()
    orb_i = pair_v[pl.ds(0, 1), :]
    orb_j = pair_v[pl.ds(1, 1), :]
    nocc = fk.shape[0]
    orbs = lax.broadcasted_iota(jnp.int32, (nocc, pairs), 0)
    at_i = orbs == orb_i
    at_j = orbs == orb_j
    tn = (((0,), (0,)), ((), ()))
    f_i = lax.dot_general(fk[...], jnp.where(at_i, 1.0, 0.0).astype(BF16), tn, preferred_element_type=F32)
    f_j = lax.dot_general(fk[...], jnp.where(at_j, 1.0, 0.0).astype(BF16), tn, preferred_element_type=F32)

    def entry(mask, table):
        return jnp.sum(jnp.where(mask, table, 0.0), axis=0, keepdims=True)

    pad = jnp.zeros((1, LANES - pairs), F32)
    mix = [jnp.zeros((1, pairs), F32) for _ in range(n_grp)]
    for e in range(cpl_v.shape[0]):
        k_orb = cpl_v[e, pl.ds(0, 1), :]
        l_orb = cpl_v[e, pl.ds(1, 1), :]
        f_ik = entry(orbs == k_orb, f_i)
        f_jl = entry(orbs == l_orb, f_j)
        w = jnp.where((l_orb == orb_j) & (k_orb != orb_i), f_ik, 0.0)
        w = w + jnp.where((k_orb == orb_i) & (l_orb != orb_j), f_jl, 0.0)
        slot = slot_v[pl.ds(e, 1), :]
        for s in range(n_grp):
            mix[s] = mix[s] + jnp.where(slot == s, w, 0.0)
    diag = entry(at_i, f_i) + entry(at_j, f_j)
    for s in range(n_grp):
        wt_v[pl.ds(s, 1), :] = jnp.concatenate([mix[s], pad], axis=1)
    wt_v[pl.ds(n_grp, 1), :] = jnp.concatenate([diag, pad], axis=1)
    wt_copy = pltpu.make_async_copy(wt_v, wt_s, wt_sem)
    wt_copy.start()
    wt_copy.wait()
    met_copy.wait()

    def wait_blocks(c):
        c0, c1 = chunks[c]
        ref = pk.at[pl.ds(0, n_dev - 1), pl.ds(c0, c1 - c0), :]
        own_copy(c).wait()
        pltpu.make_async_copy(ref, ref, a_recv.at[c]).wait()

    def fit(c):
        c0, c1 = chunks[c]
        w = c1 - c0
        left = it[:, c0:c1, :].reshape(n_grp * w, n_aux * rows)
        tile = 2 * LANES

        @pl.loop(0, (n_aux * rows) // tile)
        def _(t):
            q0 = pl.multiple_of(t * tile, tile)
            f = lax.dot_general(left, met[pl.ds(q0, tile), :], NT, preferred_element_type=F32)
            ft[:, pl.ds(c0, w), pl.ds(q0, tile)] = f.astype(BF16).reshape(n_grp, w, tile)

    def gram(c):
        c0, c1 = chunks[c]
        w = c1 - c0
        left = ft[:, c0:c1, :].reshape(n_grp * w, n_aux * rows)

        @pl.loop(0, n_grp)
        def _(o):
            k = lax.dot_general(left, ft[o, 0:c1, :], NT, preferred_element_type=F32)
            for s in range(n_grp):
                gs[c][s * n_grp + o, :, 0:c1] = k[s * w:(s + 1) * w]

    def slots(p):
        return pair_s[0, p] // group_orbs, pair_s[1, p] // group_orbs

    def strip(c, p, part, incoming):
        c0, c1 = chunks[c]
        width = c0 if part else c1
        i, j = slots(p)
        which = j * n_grp + i if part else i * n_grp + j
        kmat = gs[c][which, :, 0:width]
        denom = vsum[c0:c1, 0:width] - wt_s[n_grp, p]
        if incoming is None:
            return -(kmat / denom)
        term = wt_s[0, p] * incoming[0, part, :, 0:width].astype(F32)
        for s in range(1, n_grp):
            term = term + wt_s[s, p] * incoming[s, part, :, 0:width].astype(F32)
        return (term - kmat) / denom

    def x_copy(c, r, d):
        return pltpu.make_async_remote_copy(
            src_ref=tx[c].at[r, d], dst_ref=rx[c].at[r, g],
            send_sem=x_send.at[r, c], recv_sem=x_recv.at[r, c],
            device_id=(a, lax.rem(g + d, n_grp)), device_id_type=MESH,
        )

    def exchange(c, r):
        c0, c1 = chunks[c]
        incoming = None if r == 0 else rx[c].at[r - 1]
        for d in list(range(1, n_grp)) + [0]:
            p = send_pair[0, lax.rem(g + d, n_grp)]
            for part in range(2 if c0 else 1):
                width = c0 if part else c1
                v = strip(c, p, part, incoming).astype(BF16)
                if d:
                    tx[c][r, d, part, :, 0:width] = v
                else:
                    rx[c][r, g, part, :, 0:width] = v
            if d:
                x_copy(c, r, d).start()

    def wait_exchange(c, r):
        ref = tx[c].at[r, pl.ds(1, n_grp - 1)]
        pltpu.make_async_copy(ref, ref, x_recv.at[r, c]).wait()

    def finish(c):
        c0, c1 = chunks[c]
        incoming = rx[c].at[ITERS - 1]

        @pl.loop(0, pairs)
        def _(p):
            out[p, c0:c1, 0:c1] = strip(c, p, 0, incoming)
            if c0:
                out[p, 0:c0, c0:c1] = jnp.transpose(strip(c, p, 1, incoming))

    n = len(chunks)
    for t in range(n + ITERS):
        if t < n:
            wait_blocks(t)
            if t + 2 < n:
                send_chunk(t + 2)
            fit(t)
            gram(t)
            exchange(t, 0)
        for r in range(1, ITERS + 1):
            c = t - r
            if 0 <= c < n:
                wait_exchange(c, r - 1)
                if r < ITERS:
                    exchange(c, r)
                else:
                    finish(c)

    ref = idx_rx.at[pl.ds(1, n_aux - 1)]
    pltpu.make_async_copy(ref, ref, idx_send).wait()
    for c, (c0, c1) in enumerate(chunks):
        ref = pk.at[pl.ds(0, n_dev - 1), pl.ds(c0, c1 - c0), :]
        pltpu.make_async_copy(ref, ref, a_send.at[c]).wait()
        for r in range(ITERS):
            ref = tx[c].at[r, pl.ds(1, n_grp - 1)]
            pltpu.make_async_copy(ref, ref, x_send.at[r, c]).wait()


def fused(integrals, metric, fock, virt_energy, send_orb, pair_orb, send_pair, cpl_slot, cpl_orb):
    rows, group_orbs, nv = integrals.shape
    n_aux = lax.axis_size("aux")
    n_grp = lax.axis_size("grp")
    naux = n_aux * rows
    od = group_orbs // n_aux
    pairs = pair_orb.shape[0]
    chunks = chunks_of(nv)
    n = len(chunks)
    dims = (n_aux, n_grp, rows, od, nv, pairs, group_orbs, chunks)
    dma = pltpu.SemaphoreType.DMA
    hbm = pl.BlockSpec(memory_space=pltpu.HBM)
    vmem = pl.BlockSpec(memory_space=pltpu.VMEM)
    smem = pl.BlockSpec(memory_space=pltpu.SMEM)
    parts = [(2 if c0 else 1, c1 - c0, up(c1)) for c0, c1 in chunks]
    return pl.pallas_call(
        functools.partial(fused_kernel, dims),
        out_shape=jax.ShapeDtypeStruct((pairs, nv, nv), F32),
        in_specs=[hbm, hbm, hbm, vmem, smem, smem, vmem, smem, vmem, vmem],
        out_specs=vmem,
        scratch_shapes=[
            pltpu.VMEM((n_aux, rows, od, nv), BF16),
            pltpu.VMEM((n_aux * n_grp, nv, rows), BF16),
            pltpu.VMEM((n_grp, nv, naux), BF16),
            pltpu.VMEM((n_grp, nv, naux), BF16),
            pltpu.VMEM(metric.shape, BF16),
            pltpu.VMEM(fock.shape, BF16),
            pltpu.VMEM((nv, nv), F32),
            pltpu.VMEM((8, LANES), jnp.int32),
            pltpu.VMEM((n_aux, 8, LANES), jnp.int32),
            pltpu.VMEM((8, LANES), F32),
            pltpu.SMEM((8, LANES), F32),
            [pltpu.VMEM((n_grp * n_grp, c1 - c0, up(c1)), F32) for c0, c1 in chunks],
            [pltpu.VMEM((ITERS, n_grp, *p), BF16) for p in parts],
            [pltpu.VMEM((ITERS, n_grp, *p), BF16) for p in parts],
            dma((n_aux,)), dma, dma, dma, dma, dma, dma((n,)),
            dma((n,)), dma((n,)), dma((ITERS, n)), dma((ITERS, n)),
        ],
        compiler_params=pltpu.CompilerParams(
            collective_id=0, has_side_effects=True, vmem_limit_bytes=52 * 1024 * 1024
        ),
    )(
        integrals, metric, fock, virt_energy[None, :], send_orb, pair_orb.T, pair_orb.T, send_pair,
        cpl_slot.T, jnp.transpose(cpl_orb, (1, 2, 0)),
    )


def fits_fused(integrals, pair_orb):
    rows, group_orbs, nv = integrals.shape
    n_aux, n_grp = lax.axis_size("aux"), lax.axis_size("grp")
    return (
        rows % LANES == 0
        and nv % (2 * LANES) == 0
        and n_aux % 2 == 0
        and group_orbs == 16 * n_aux
        and n_grp < 8
        and n_grp * n_grp <= pair_orb.shape[0] <= LANES
    )


def final_kernel(idx_i, idx_j, mixing, diag, fit_ref, ve_col, ve_row, inc_ref, out_ref):
    p = pl.program_id(0)
    kmat = lax.dot_general(
        fit_ref[idx_i[p]],
        fit_ref[idx_j[p]],
        (((0,), (0,)), ((), ())),
        preferred_element_type=jnp.float32,
    )
    term = mixing[p, 0] * inc_ref[0].astype(jnp.float32)
    for s in range(1, inc_ref.shape[0]):
        term = term + mixing[p, s] * inc_ref[s].astype(jnp.float32)
    denom = (ve_col[...] + ve_row[...]) - diag[p]
    out_ref[0] = (term - kmat) / denom


def final_call(idx_i, idx_j, mixing, diag, fitted, virt_energy, incoming):
    pairs = idx_i.shape[0]
    nv = virt_energy.shape[0]
    whole = pl.BlockSpec(memory_space=pltpu.VMEM)
    return pl.pallas_call(
        final_kernel,
        out_shape=jax.ShapeDtypeStruct((pairs, nv, nv), jnp.float32),
        grid_spec=pltpu.PrefetchScalarGridSpec(
            num_scalar_prefetch=4,
            grid=(pairs,),
            in_specs=[whole, whole, whole, whole],
            out_specs=pl.BlockSpec((1, nv, nv), lambda p, *_: (p, 0, 0)),
        ),
    )(idx_i, idx_j, mixing, diag, fitted, virt_energy[:, None], virt_energy[None, :], incoming)


def stepwise(
    integrals, metric, fock, virt_energy, send_orb, pair_orb, send_pair, cpl_slot, cpl_orb
):
    rows, group_orbs, nv = integrals.shape
    n_aux = lax.axis_size("aux")
    n_grp = lax.axis_size("grp")
    orb_dev = group_orbs // n_aux
    spread = jnp.broadcast_to(send_orb, (n_aux, n_grp))
    wanted = lax.all_to_all(spread, "aux", split_axis=0, concat_axis=0, tiled=True)
    idx = (jnp.arange(n_aux, dtype=jnp.int32)[:, None] * orb_dev + wanted).reshape(-1)
    packed = jnp.transpose(jnp.take(integrals, idx, axis=1, mode="clip"), (1, 0, 2))
    block = lax.all_to_all(packed, ("aux", "grp"), split_axis=0, concat_axis=0, tiled=True)
    block = block.reshape(n_aux, n_grp, rows, nv)
    block = jnp.transpose(block, (0, 2, 1, 3)).reshape(n_aux * rows, n_grp * nv)
    fitted = jnp.dot(metric, block, preferred_element_type=jnp.float32).astype(jnp.bfloat16)
    fitted = jnp.transpose(fitted.reshape(n_aux * rows, n_grp, nv), (1, 0, 2))

    orb_i = pair_orb[:, 0]
    orb_j = pair_orb[:, 1]
    idx_i = orb_i // group_orbs
    idx_j = orb_j // group_orbs
    diag_sum = fock[orb_i, orb_i].astype(jnp.float32) + fock[orb_j, orb_j].astype(jnp.float32)
    k_orb = cpl_orb[:, :, 0]
    l_orb = cpl_orb[:, :, 1]
    first = (l_orb == orb_j[:, None]) & (k_orb != orb_i[:, None])
    second = (k_orb == orb_i[:, None]) & (l_orb != orb_j[:, None])
    f_ik = fock[orb_i[:, None], k_orb].astype(jnp.float32)
    f_jl = fock[orb_j[:, None], l_orb].astype(jnp.float32)
    weight = jnp.where(first, f_ik, 0.0) + jnp.where(second, f_jl, 0.0)
    onehot = cpl_slot[:, :, None] == jnp.arange(n_grp, dtype=jnp.int32)[None, None, :]
    mixing = jnp.sum(jnp.where(onehot, weight[:, :, None], 0.0), axis=1)

    sent = send_pair[0]
    zeros = jnp.zeros((n_grp, nv, nv), jnp.bfloat16)
    s_i, s_j, s_mix, s_diag = idx_i[sent], idx_j[sent], mixing[sent], diag_sum[sent]
    incoming = zeros
    for step in range(ITERS):
        amps = final_call(s_i, s_j, s_mix, s_diag, fitted, virt_energy, incoming)
        incoming = lax.all_to_all(
            amps.astype(jnp.bfloat16), "grp", split_axis=0, concat_axis=0, tiled=True
        )
    return final_call(idx_i, idx_j, mixing, diag_sum, fitted, virt_energy, incoming)


def on_device(*args):
    return fused(*args) if fits_fused(args[0], args[5]) else stepwise(*args)


def solution(mesh):
    in_specs = (
        P("aux", "grp", None),
        P(),
        P(),
        P(),
        P(("aux", "grp"), None),
        P(("aux", "grp"), None),
        P(("aux", "grp"), None),
        P(("aux", "grp"), None),
        P(("aux", "grp"), None, None),
    )
    out_specs = P(("aux", "grp"), None, None)
    return jax.shard_map(
        on_device, mesh=mesh, in_specs=in_specs, out_specs=out_specs, check_vma=False
    )
```

```python
import functools

import jax
import jax.numpy as jnp
from jax import lax
from jax.experimental import pallas as pl
from jax.experimental.pallas import tpu as pltpu
from jax.sharding import PartitionSpec as P

ITERS = 2
MESH = pl.DeviceIdType.MESH
F32 = jnp.float32
BF16 = jnp.bfloat16
NT = (((1,), (1,)), ((), ()))
LANES = 128


def chunks_of(nv):
    cuts = [0, nv // 2, nv * 3 // 4, nv * 7 // 8, nv]
    return list(zip(cuts[:-1], cuts[1:]))


def up(n):
    return -(-n // LANES) * LANES


def fused_kernel(
    dims,
    integrals, metric, fock, ve_hbm, orb_hbm, pair_hbm, mine_hbm, slot_hbm, cpl_hbm,
    out,
    raw, pk, it, ft, met, fk, vsum, idx_tx, idx_rx, wt_v, wt_s,
    ve_row, send_orb, pair_s, pair_v, send_pair, slot_v, cpl_v,
    gs, tx, rx,
    raw_sem, met_sem, fk_sem, wt_sem, small_sem, idx_send, idx_recv, own_sem,
    a_send, a_recv, x_send, x_recv,
):
    n_aux, n_grp, rows, od, nv, pairs, group_orbs, chunks = dims
    a = lax.axis_index("aux")
    g = lax.axis_index("grp")
    n_dev = n_aux * n_grp
    half = n_aux // 2

    def col_of(k):
        off = half + jnp.where(k % 2 == 0, k // 2, -((k + 1) // 2))
        return lax.rem(a + off, n_aux)

    def raw_copy(k, col):
        first = pl.multiple_of(col * od, od)
        return pltpu.make_async_copy(integrals.at[:, pl.ds(first, od), :], raw.at[k], raw_sem.at[k])

    small = [
        pltpu.make_async_copy(src, dst, small_sem.at[k])
        for k, (src, dst) in enumerate([
            (orb_hbm, send_orb), (mine_hbm, send_pair), (pair_hbm, pair_s), (pair_hbm, pair_v),
            (slot_hbm, slot_v), (cpl_hbm, cpl_v), (ve_hbm, ve_row),
        ])
    ]
    for copy in small:
        copy.start()
    barrier = pltpu.get_barrier_semaphore()

    @pl.loop(1, n_dev)
    def _(k):
        t = lax.rem(a * n_grp + g + k, n_dev)
        pl.semaphore_signal(barrier, inc=1, device_id=(t // n_grp, t % n_grp), device_id_type=MESH)

    @pl.loop(0, n_aux)
    def _(k):
        raw_copy(k, col_of(k)).start()

    met_copy = pltpu.make_async_copy(metric, met, met_sem)
    fk_copy = pltpu.make_async_copy(fock, fk, fk_sem)
    met_copy.start()
    fk_copy.start()
    small[0].wait()
    for s in range(n_grp):
        idx_tx[pl.ds(s, 1), :] = jnp.full((1, LANES), send_orb[0, s], jnp.int32)
        idx_rx[a, pl.ds(s, 1), :] = jnp.full((1, LANES), send_orb[0, s], jnp.int32)

    pl.semaphore_wait(barrier, n_dev - 1)

    def idx_copy(k):
        t = lax.rem(a + k, n_aux)
        return pltpu.make_async_remote_copy(
            src_ref=idx_tx, dst_ref=idx_rx.at[a], send_sem=idx_send, recv_sem=idx_recv,
            device_id=(t, g), device_id_type=MESH,
        )

    @pl.loop(1, n_aux)
    def _(k):
        idx_copy(k).start()

    idx_all = pltpu.make_async_copy(idx_rx.at[pl.ds(1, n_aux - 1)], idx_rx.at[pl.ds(1, n_aux - 1)], idx_recv)
    idx_all.wait()

    def block_copy(c, col, grp):
        c0, c1 = chunks[c]
        lane0 = pl.multiple_of(a * rows, rows)
        return pltpu.make_async_remote_copy(
            src_ref=pk.at[col * n_grp + grp, pl.ds(c0, c1 - c0), :],
            dst_ref=it.at[g, pl.ds(c0, c1 - c0), pl.ds(lane0, rows)],
            send_sem=a_send.at[c], recv_sem=a_recv.at[c],
            device_id=(col, grp), device_id_type=MESH,
        )

    def own_copy(c):
        c0, c1 = chunks[c]
        lane0 = pl.multiple_of(a * rows, rows)
        return pltpu.make_async_copy(
            pk.at[a * n_grp + g, pl.ds(c0, c1 - c0), :],
            it.at[g, pl.ds(c0, c1 - c0), pl.ds(lane0, rows)],
            own_sem.at[c],
        )

    def send_far(c, k):
        col = col_of(k)
        for d in range(n_grp):
            block_copy(c, col, lax.rem(g + d, n_grp)).start()

    def send_own(c):
        for d in range(1, n_grp):
            block_copy(c, a, lax.rem(g + d, n_grp)).start()
        own_copy(c).start()

    step = 2 * LANES // od
    lane = lax.broadcasted_iota(jnp.int32, (step, 2 * LANES), 1)
    row = lax.broadcasted_iota(jnp.int32, (step, 2 * LANES), 0)

    def select(k, col):
        raw_copy(k, col).wait()
        pick = []
        for s in range(n_grp):
            v = idx_rx[col, pl.ds(s, 1), :]
            v = jnp.broadcast_to(jnp.concatenate([v, v], axis=1), (step, 2 * LANES))
            pick.append(jnp.where(lane == row * od + v, 1.0, 0.0))
        sel = jnp.concatenate(pick, axis=0).astype(BF16)
        parts = []
        for t in range(rows // step):
            x = raw[k, t * step:(t + 1) * step].reshape(step * od, nv)
            parts.append(jnp.dot(sel, x, preferred_element_type=F32))
        for s in range(n_grp):
            blk = jnp.concatenate([p[s * step:(s + 1) * step] for p in parts], axis=0)
            pk[col * n_grp + s] = jnp.transpose(blk).astype(BF16)

    @pl.loop(0, n_aux - 1)
    def _(k):
        select(k, col_of(k))
        send_far(0, k)

    select(n_aux - 1, a)
    send_own(0)

    def send_chunk(c):
        @pl.loop(0, n_aux - 1)
        def _(k):
            send_far(c, k)

        send_own(c)

    send_chunk(1)

    for copy in small[1:]:
        copy.wait()
    ve = ve_row[...]
    vb = jnp.broadcast_to(ve, (nv, nv))
    vsum[...] = jnp.transpose(vb) + vb

    fk_copy.wait()
    orb_i = pair_v[pl.ds(0, 1), :]
    orb_j = pair_v[pl.ds(1, 1), :]
    nocc = fk.shape[0]
    orbs = lax.broadcasted_iota(jnp.int32, (nocc, pairs), 0)
    at_i = orbs == orb_i
    at_j = orbs == orb_j
    tn = (((0,), (0,)), ((), ()))
    f_i = lax.dot_general(fk[...], jnp.where(at_i, 1.0, 0.0).astype(BF16), tn, preferred_element_type=F32)
    f_j = lax.dot_general(fk[...], jnp.where(at_j, 1.0, 0.0).astype(BF16), tn, preferred_element_type=F32)

    def entry(mask, table):
        return jnp.sum(jnp.where(mask, table, 0.0), axis=0, keepdims=True)

    pad = jnp.zeros((1, LANES - pairs), F32)
    mix = [jnp.zeros((1, pairs), F32) for _ in range(n_grp)]
    for e in range(cpl_v.shape[0]):
        k_orb = cpl_v[e, pl.ds(0, 1), :]
        l_orb = cpl_v[e, pl.ds(1, 1), :]
        f_ik = entry(orbs == k_orb, f_i)
        f_jl = entry(orbs == l_orb, f_j)
        w = jnp.where((l_orb == orb_j) & (k_orb != orb_i), f_ik, 0.0)
        w = w + jnp.where((k_orb == orb_i) & (l_orb != orb_j), f_jl, 0.0)
        slot = slot_v[pl.ds(e, 1), :]
        for s in range(n_grp):
            mix[s] = mix[s] + jnp.where(slot == s, w, 0.0)
    diag = entry(at_i, f_i) + entry(at_j, f_j)
    for s in range(n_grp):
        wt_v[pl.ds(s, 1), :] = jnp.concatenate([mix[s], pad], axis=1)
    wt_v[pl.ds(n_grp, 1), :] = jnp.concatenate([diag, pad], axis=1)
    wt_copy = pltpu.make_async_copy(wt_v, wt_s, wt_sem)
    wt_copy.start()
    wt_copy.wait()
    met_copy.wait()

    def wait_blocks(c):
        c0, c1 = chunks[c]
        ref = pk.at[pl.ds(0, n_dev - 1), pl.ds(c0, c1 - c0), :]
        own_copy(c).wait()
        pltpu.make_async_copy(ref, ref, a_recv.at[c]).wait()

    def fit(c):
        c0, c1 = chunks[c]
        w = c1 - c0
        left = it[:, c0:c1, :].reshape(n_grp * w, n_aux * rows)
        tile = 2 * LANES

        @pl.loop(0, (n_aux * rows) // tile)
        def _(t):
            q0 = pl.multiple_of(t * tile, tile)
            f = lax.dot_general(left, met[pl.ds(q0, tile), :], NT, preferred_element_type=F32)
            ft[:, pl.ds(c0, w), pl.ds(q0, tile)] = f.astype(BF16).reshape(n_grp, w, tile)

    def gram(c):
        c0, c1 = chunks[c]
        w = c1 - c0
        left = ft[:, c0:c1, :].reshape(n_grp * w, n_aux * rows)

        @pl.loop(0, n_grp)
        def _(o):
            k = lax.dot_general(left, ft[o, 0:c1, :], NT, preferred_element_type=F32)
            for s in range(n_grp):
                gs[c][s * n_grp + o, :, 0:c1] = k[s * w:(s + 1) * w]

    def slots(p):
        return pair_s[0, p] // group_orbs, pair_s[1, p] // group_orbs

    def strip(c, p, part, incoming):
        c0, c1 = chunks[c]
        width = c0 if part else c1
        i, j = slots(p)
        which = j * n_grp + i if part else i * n_grp + j
        kmat = gs[c][which, :, 0:width]
        denom = vsum[c0:c1, 0:width] - wt_s[n_grp, p]
        if incoming is None:
            return -(kmat / denom)
        term = wt_s[0, p] * incoming[0, part, :, 0:width].astype(F32)
        for s in range(1, n_grp):
            term = term + wt_s[s, p] * incoming[s, part, :, 0:width].astype(F32)
        return (term - kmat) / denom

    def x_copy(c, r, d):
        return pltpu.make_async_remote_copy(
            src_ref=tx[c].at[r, d], dst_ref=rx[c].at[r, g],
            send_sem=x_send.at[r, c], recv_sem=x_recv.at[r, c],
            device_id=(a, lax.rem(g + d, n_grp)), device_id_type=MESH,
        )

    def exchange(c, r):
        c0, c1 = chunks[c]
        incoming = None if r == 0 else rx[c].at[r - 1]
        for d in list(range(1, n_grp)) + [0]:
            p = send_pair[0, lax.rem(g + d, n_grp)]
            for part in range(2 if c0 else 1):
                width = c0 if part else c1
                v = strip(c, p, part, incoming).astype(BF16)
                if d:
                    tx[c][r, d, part, :, 0:width] = v
                else:
                    rx[c][r, g, part, :, 0:width] = v
            if d:
                x_copy(c, r, d).start()

    def wait_exchange(c, r):
        ref = tx[c].at[r, pl.ds(1, n_grp - 1)]
        pltpu.make_async_copy(ref, ref, x_recv.at[r, c]).wait()

    def finish(c):
        c0, c1 = chunks[c]
        incoming = rx[c].at[ITERS - 1]

        @pl.loop(0, pairs)
        def _(p):
            out[p, c0:c1, 0:c1] = strip(c, p, 0, incoming)
            if c0:
                out[p, 0:c0, c0:c1] = jnp.transpose(strip(c, p, 1, incoming))

    n = len(chunks)
    for t in range(n + ITERS):
        if t < n:
            wait_blocks(t)
            if t + 2 < n:
                send_chunk(t + 2)
            fit(t)
            gram(t)
            exchange(t, 0)
        for r in range(1, ITERS + 1):
            c = t - r
            if 0 <= c < n:
                wait_exchange(c, r - 1)
                if r < ITERS:
                    exchange(c, r)
                else:
                    finish(c)

    ref = idx_rx.at[pl.ds(1, n_aux - 1)]
    pltpu.make_async_copy(ref, ref, idx_send).wait()
    for c, (c0, c1) in enumerate(chunks):
        ref = pk.at[pl.ds(0, n_dev - 1), pl.ds(c0, c1 - c0), :]
        pltpu.make_async_copy(ref, ref, a_send.at[c]).wait()
        for r in range(ITERS):
            ref = tx[c].at[r, pl.ds(1, n_grp - 1)]
            pltpu.make_async_copy(ref, ref, x_send.at[r, c]).wait()


def fused(integrals, metric, fock, virt_energy, send_orb, pair_orb, send_pair, cpl_slot, cpl_orb):
    rows, group_orbs, nv = integrals.shape
    n_aux = lax.axis_size("aux")
    n_grp = lax.axis_size("grp")
    naux = n_aux * rows
    od = group_orbs // n_aux
    pairs = pair_orb.shape[0]
    chunks = chunks_of(nv)
    n = len(chunks)
    dims = (n_aux, n_grp, rows, od, nv, pairs, group_orbs, chunks)
    dma = pltpu.SemaphoreType.DMA
    hbm = pl.BlockSpec(memory_space=pltpu.HBM)
    vmem = pl.BlockSpec(memory_space=pltpu.VMEM)

    def here(x):
        return pltpu.with_memory_space_constraint(x, pltpu.HBM)

    small = [
        virt_energy[None, :], send_orb, pair_orb.T, send_pair,
        cpl_slot.T, jnp.transpose(cpl_orb, (1, 2, 0)),
    ]
    parts = [(2 if c0 else 1, c1 - c0, up(c1)) for c0, c1 in chunks]
    return pl.pallas_call(
        functools.partial(fused_kernel, dims),
        out_shape=pltpu.VMEM((pairs, nv, nv), F32),
        in_specs=[hbm] * 9,
        out_specs=vmem,
        scratch_shapes=[
            pltpu.VMEM((n_aux, rows, od, nv), BF16),
            pltpu.VMEM((n_aux * n_grp, nv, rows), BF16),
            pltpu.VMEM((n_grp, nv, naux), BF16),
            pltpu.VMEM((n_grp, nv, naux), BF16),
            pltpu.VMEM(metric.shape, BF16),
            pltpu.VMEM(fock.shape, BF16),
            pltpu.VMEM((nv, nv), F32),
            pltpu.VMEM((8, LANES), jnp.int32),
            pltpu.VMEM((n_aux, 8, LANES), jnp.int32),
            pltpu.VMEM((8, LANES), F32),
            pltpu.SMEM((8, LANES), F32),
            pltpu.VMEM((1, nv), F32),
            pltpu.SMEM(send_orb.shape, jnp.int32),
            pltpu.SMEM((2, pairs), jnp.int32),
            pltpu.VMEM((2, pairs), jnp.int32),
            pltpu.SMEM(send_pair.shape, jnp.int32),
            pltpu.VMEM(small[4].shape, jnp.int32),
            pltpu.VMEM(small[5].shape, jnp.int32),
            [pltpu.VMEM((n_grp * n_grp, c1 - c0, up(c1)), F32) for c0, c1 in chunks],
            [pltpu.VMEM((ITERS, n_grp, *p), BF16) for p in parts],
            [pltpu.VMEM((ITERS, n_grp, *p), BF16) for p in parts],
            dma((n_aux,)), dma, dma, dma, dma((7,)), dma, dma, dma((n,)),
            dma((n,)), dma((n,)), dma((ITERS, n)), dma((ITERS, n)),
        ],
        compiler_params=pltpu.CompilerParams(
            collective_id=0, has_side_effects=True, vmem_limit_bytes=52 * 1024 * 1024
        ),
    )(*[here(x) for x in [integrals, metric, fock] + small])


def fits_fused(integrals, pair_orb):
    rows, group_orbs, nv = integrals.shape
    n_aux, n_grp = lax.axis_size("aux"), lax.axis_size("grp")
    return (
        rows % LANES == 0
        and nv % (2 * LANES) == 0
        and n_aux % 2 == 0
        and group_orbs == 16 * n_aux
        and n_grp < 8
        and n_grp * n_grp <= pair_orb.shape[0] <= LANES
    )


def final_kernel(idx_i, idx_j, mixing, diag, fit_ref, ve_col, ve_row, inc_ref, out_ref):
    p = pl.program_id(0)
    kmat = lax.dot_general(
        fit_ref[idx_i[p]],
        fit_ref[idx_j[p]],
        (((0,), (0,)), ((), ())),
        preferred_element_type=jnp.float32,
    )
    term = mixing[p, 0] * inc_ref[0].astype(jnp.float32)
    for s in range(1, inc_ref.shape[0]):
        term = term + mixing[p, s] * inc_ref[s].astype(jnp.float32)
    denom = (ve_col[...] + ve_row[...]) - diag[p]
    out_ref[0] = (term - kmat) / denom


def final_call(idx_i, idx_j, mixing, diag, fitted, virt_energy, incoming):
    pairs = idx_i.shape[0]
    nv = virt_energy.shape[0]
    whole = pl.BlockSpec(memory_space=pltpu.VMEM)
    return pl.pallas_call(
        final_kernel,
        out_shape=jax.ShapeDtypeStruct((pairs, nv, nv), jnp.float32),
        grid_spec=pltpu.PrefetchScalarGridSpec(
            num_scalar_prefetch=4,
            grid=(pairs,),
            in_specs=[whole, whole, whole, whole],
            out_specs=pl.BlockSpec((1, nv, nv), lambda p, *_: (p, 0, 0)),
        ),
    )(idx_i, idx_j, mixing, diag, fitted, virt_energy[:, None], virt_energy[None, :], incoming)


def stepwise(
    integrals, metric, fock, virt_energy, send_orb, pair_orb, send_pair, cpl_slot, cpl_orb
):
    rows, group_orbs, nv = integrals.shape
    n_aux = lax.axis_size("aux")
    n_grp = lax.axis_size("grp")
    orb_dev = group_orbs // n_aux
    spread = jnp.broadcast_to(send_orb, (n_aux, n_grp))
    wanted = lax.all_to_all(spread, "aux", split_axis=0, concat_axis=0, tiled=True)
    idx = (jnp.arange(n_aux, dtype=jnp.int32)[:, None] * orb_dev + wanted).reshape(-1)
    packed = jnp.transpose(jnp.take(integrals, idx, axis=1, mode="clip"), (1, 0, 2))
    block = lax.all_to_all(packed, ("aux", "grp"), split_axis=0, concat_axis=0, tiled=True)
    block = block.reshape(n_aux, n_grp, rows, nv)
    block = jnp.transpose(block, (0, 2, 1, 3)).reshape(n_aux * rows, n_grp * nv)
    fitted = jnp.dot(metric, block, preferred_element_type=jnp.float32).astype(jnp.bfloat16)
    fitted = jnp.transpose(fitted.reshape(n_aux * rows, n_grp, nv), (1, 0, 2))

    orb_i = pair_orb[:, 0]
    orb_j = pair_orb[:, 1]
    idx_i = orb_i // group_orbs
    idx_j = orb_j // group_orbs
    diag_sum = fock[orb_i, orb_i].astype(jnp.float32) + fock[orb_j, orb_j].astype(jnp.float32)
    k_orb = cpl_orb[:, :, 0]
    l_orb = cpl_orb[:, :, 1]
    first = (l_orb == orb_j[:, None]) & (k_orb != orb_i[:, None])
    second = (k_orb == orb_i[:, None]) & (l_orb != orb_j[:, None])
    f_ik = fock[orb_i[:, None], k_orb].astype(jnp.float32)
    f_jl = fock[orb_j[:, None], l_orb].astype(jnp.float32)
    weight = jnp.where(first, f_ik, 0.0) + jnp.where(second, f_jl, 0.0)
    onehot = cpl_slot[:, :, None] == jnp.arange(n_grp, dtype=jnp.int32)[None, None, :]
    mixing = jnp.sum(jnp.where(onehot, weight[:, :, None], 0.0), axis=1)

    sent = send_pair[0]
    zeros = jnp.zeros((n_grp, nv, nv), jnp.bfloat16)
    s_i, s_j, s_mix, s_diag = idx_i[sent], idx_j[sent], mixing[sent], diag_sum[sent]
    incoming = zeros
    for step in range(ITERS):
        amps = final_call(s_i, s_j, s_mix, s_diag, fitted, virt_energy, incoming)
        incoming = lax.all_to_all(
            amps.astype(jnp.bfloat16), "grp", split_axis=0, concat_axis=0, tiled=True
        )
    return final_call(idx_i, idx_j, mixing, diag_sum, fitted, virt_energy, incoming)


def on_device(*args):
    return fused(*args) if fits_fused(args[0], args[5]) else stepwise(*args)


def solution(mesh):
    in_specs = (
        P("aux", "grp", None),
        P(),
        P(),
        P(),
        P(("aux", "grp"), None),
        P(("aux", "grp"), None),
        P(("aux", "grp"), None),
        P(("aux", "grp"), None),
        P(("aux", "grp"), None, None),
    )
    out_specs = P(("aux", "grp"), None, None)
    return jax.shard_map(
        on_device, mesh=mesh, in_specs=in_specs, out_specs=out_specs, check_vma=False
    )
```

```python
import functools

import jax
import jax.numpy as jnp
from jax import lax
from jax.experimental import pallas as pl
from jax.experimental.pallas import tpu as pltpu
from jax.sharding import PartitionSpec as P

ITERS = 2
MESH = pl.DeviceIdType.MESH
F32 = jnp.float32
BF16 = jnp.bfloat16
NT = (((1,), (1,)), ((), ()))
LANES = 128


def chunks_of(nv):
    cuts = [0, nv // 2, nv * 3 // 4, nv * 7 // 8, nv]
    return list(zip(cuts[:-1], cuts[1:]))


def up(n):
    return -(-n // LANES) * LANES


def fused_kernel(
    dims,
    integrals, metric, fock, ve_hbm, orb_hbm, pair_hbm, mine_hbm, slot_hbm, cpl_hbm,
    out,
    raw, pk, it, ft, met, met_t, fk, vsum, idx_tx, idx_rx, wt_v, wt_s,
    ve_row, send_orb, pair_s, pair_v, send_pair, slot_v, cpl_v,
    gs, tx, rx,
    raw_sem, met_sem, fk_sem, wt_sem, small_sem, idx_send, idx_recv, own_sem,
    a_send, a_recv, x_send, x_recv,
):
    n_aux, n_grp, rows, od, nv, pairs, group_orbs, chunks = dims
    a = lax.axis_index("aux")
    g = lax.axis_index("grp")
    n_dev = n_aux * n_grp
    half = n_aux // 2

    def col_of(k):
        off = half + jnp.where(k % 2 == 0, k // 2, -((k + 1) // 2))
        return lax.rem(a + off, n_aux)

    def raw_copy(k, col):
        first = pl.multiple_of(col * od, od)
        return pltpu.make_async_copy(integrals.at[:, pl.ds(first, od), :], raw.at[k], raw_sem.at[k])

    small = [
        pltpu.make_async_copy(src, dst, small_sem.at[k])
        for k, (src, dst) in enumerate([
            (orb_hbm, send_orb), (mine_hbm, send_pair), (pair_hbm, pair_s), (pair_hbm, pair_v),
            (slot_hbm, slot_v), (cpl_hbm, cpl_v), (ve_hbm, ve_row),
        ])
    ]
    for copy in small:
        copy.start()
    barrier = pltpu.get_barrier_semaphore()

    @pl.loop(1, n_dev)
    def _(k):
        t = lax.rem(a * n_grp + g + k, n_dev)
        pl.semaphore_signal(barrier, inc=1, device_id=(t // n_grp, t % n_grp), device_id_type=MESH)

    @pl.loop(0, n_aux)
    def _(k):
        raw_copy(k, col_of(k)).start()

    met_copy = pltpu.make_async_copy(metric, met, met_sem)
    fk_copy = pltpu.make_async_copy(fock, fk, fk_sem)
    met_copy.start()
    fk_copy.start()
    small[0].wait()
    for s in range(n_grp):
        idx_tx[pl.ds(s, 1), :] = jnp.full((1, LANES), send_orb[0, s], jnp.int32)
        idx_rx[a, pl.ds(s, 1), :] = jnp.full((1, LANES), send_orb[0, s], jnp.int32)

    pl.semaphore_wait(barrier, n_dev - 1)

    def idx_copy(k):
        t = lax.rem(a + k, n_aux)
        return pltpu.make_async_remote_copy(
            src_ref=idx_tx, dst_ref=idx_rx.at[a], send_sem=idx_send, recv_sem=idx_recv,
            device_id=(t, g), device_id_type=MESH,
        )

    @pl.loop(1, n_aux)
    def _(k):
        idx_copy(k).start()

    idx_all = pltpu.make_async_copy(idx_rx.at[pl.ds(1, n_aux - 1)], idx_rx.at[pl.ds(1, n_aux - 1)], idx_recv)
    idx_all.wait()

    def block_copy(c, col, grp):
        c0, c1 = chunks[c]
        lane0 = pl.multiple_of(a * rows, rows)
        return pltpu.make_async_remote_copy(
            src_ref=pk.at[col * n_grp + grp, pl.ds(c0, c1 - c0), :],
            dst_ref=it.at[g, pl.ds(c0, c1 - c0), pl.ds(lane0, rows)],
            send_sem=a_send.at[c], recv_sem=a_recv.at[c],
            device_id=(col, grp), device_id_type=MESH,
        )

    def own_copy(c):
        c0, c1 = chunks[c]
        lane0 = pl.multiple_of(a * rows, rows)
        return pltpu.make_async_copy(
            pk.at[a * n_grp + g, pl.ds(c0, c1 - c0), :],
            it.at[g, pl.ds(c0, c1 - c0), pl.ds(lane0, rows)],
            own_sem.at[c],
        )

    def send_far(c, k):
        col = col_of(k)
        for d in range(n_grp):
            block_copy(c, col, lax.rem(g + d, n_grp)).start()

    def send_own(c):
        for d in range(1, n_grp):
            block_copy(c, a, lax.rem(g + d, n_grp)).start()
        own_copy(c).start()

    step = 2 * LANES // od
    lane = lax.broadcasted_iota(jnp.int32, (step, 2 * LANES), 1)
    row = lax.broadcasted_iota(jnp.int32, (step, 2 * LANES), 0)

    def select(k, col):
        raw_copy(k, col).wait()
        pick = []
        for s in range(n_grp):
            v = idx_rx[col, pl.ds(s, 1), :]
            v = jnp.broadcast_to(jnp.concatenate([v, v], axis=1), (step, 2 * LANES))
            pick.append(jnp.where(lane == row * od + v, 1.0, 0.0))
        sel = jnp.concatenate(pick, axis=0).astype(BF16)
        parts = []
        for t in range(rows // step):
            x = raw[k, t * step:(t + 1) * step].reshape(step * od, nv)
            parts.append(jnp.dot(sel, x, preferred_element_type=F32))
        for s in range(n_grp):
            blk = jnp.concatenate([p[s * step:(s + 1) * step] for p in parts], axis=0)
            pk[col * n_grp + s] = jnp.transpose(blk).astype(BF16)

    @pl.loop(0, n_aux - 1)
    def _(k):
        select(k, col_of(k))
        send_far(0, k)

    select(n_aux - 1, a)
    send_own(0)

    def send_chunk(c):
        @pl.loop(0, n_aux - 1)
        def _(k):
            send_far(c, k)

        send_own(c)

    send_chunk(1)

    for copy in small[1:]:
        copy.wait()
    ve = ve_row[...]
    vb = jnp.broadcast_to(ve, (nv, nv))
    vsum[...] = jnp.transpose(vb) + vb

    fk_copy.wait()
    orb_i = pair_v[pl.ds(0, 1), :]
    orb_j = pair_v[pl.ds(1, 1), :]
    nocc = fk.shape[0]
    orbs = lax.broadcasted_iota(jnp.int32, (nocc, pairs), 0)
    at_i = orbs == orb_i
    at_j = orbs == orb_j
    tn = (((0,), (0,)), ((), ()))
    f_i = lax.dot_general(fk[...], jnp.where(at_i, 1.0, 0.0).astype(BF16), tn, preferred_element_type=F32)
    f_j = lax.dot_general(fk[...], jnp.where(at_j, 1.0, 0.0).astype(BF16), tn, preferred_element_type=F32)

    def entry(mask, table):
        return jnp.sum(jnp.where(mask, table, 0.0), axis=0, keepdims=True)

    pad = jnp.zeros((1, LANES - pairs), F32)
    mix = [jnp.zeros((1, pairs), F32) for _ in range(n_grp)]
    for e in range(cpl_v.shape[0]):
        k_orb = cpl_v[e, pl.ds(0, 1), :]
        l_orb = cpl_v[e, pl.ds(1, 1), :]
        f_ik = entry(orbs == k_orb, f_i)
        f_jl = entry(orbs == l_orb, f_j)
        w = jnp.where((l_orb == orb_j) & (k_orb != orb_i), f_ik, 0.0)
        w = w + jnp.where((k_orb == orb_i) & (l_orb != orb_j), f_jl, 0.0)
        slot = slot_v[pl.ds(e, 1), :]
        for s in range(n_grp):
            mix[s] = mix[s] + jnp.where(slot == s, w, 0.0)
    diag = entry(at_i, f_i) + entry(at_j, f_j)
    for s in range(n_grp):
        wt_v[pl.ds(s, 1), :] = jnp.concatenate([mix[s], pad], axis=1)
    wt_v[pl.ds(n_grp, 1), :] = jnp.concatenate([diag, pad], axis=1)
    wt_copy = pltpu.make_async_copy(wt_v, wt_s, wt_sem)
    wt_copy.start()
    wt_copy.wait()
    met_copy.wait()
    side = 2 * LANES

    @pl.loop(0, met.shape[0] // side)
    def _(t):
        q0 = pl.multiple_of(t * side, side)
        for r in range(0, met.shape[1], side):
            met_t[r:r + side, pl.ds(q0, side)] = jnp.transpose(met[pl.ds(q0, side), r:r + side])

    def wait_blocks(c):
        c0, c1 = chunks[c]
        ref = pk.at[pl.ds(0, n_dev - 1), pl.ds(c0, c1 - c0), :]
        own_copy(c).wait()
        pltpu.make_async_copy(ref, ref, a_recv.at[c]).wait()

    def fit(c):
        c0, c1 = chunks[c]
        w = c1 - c0
        left = it[:, c0:c1, :].reshape(n_grp * w, n_aux * rows)
        for q0 in range(0, n_aux * rows, side):
            f = jnp.dot(left, met_t[:, q0:q0 + side], preferred_element_type=F32)
            ft[:, pl.ds(c0, w), pl.ds(q0, side)] = f.astype(BF16).reshape(n_grp, w, side)

    def gram(c):
        c0, c1 = chunks[c]
        w = c1 - c0
        left = ft[:, c0:c1, :].reshape(n_grp * w, n_aux * rows)

        for o in range(n_grp):
            k = lax.dot_general(left, ft[o, 0:c1, :], NT, preferred_element_type=F32)
            for s in range(n_grp):
                gs[c][s * n_grp + o, :, 0:c1] = k[s * w:(s + 1) * w]

    def slots(p):
        return pair_s[0, p] // group_orbs, pair_s[1, p] // group_orbs

    def strip(c, p, part, incoming):
        c0, c1 = chunks[c]
        width = c0 if part else c1
        i, j = slots(p)
        which = j * n_grp + i if part else i * n_grp + j
        kmat = gs[c][which, :, 0:width]
        denom = vsum[c0:c1, 0:width] - wt_s[n_grp, p]
        if incoming is None:
            return -(kmat / denom)
        term = wt_s[0, p] * incoming[0, part, :, 0:width].astype(F32)
        for s in range(1, n_grp):
            term = term + wt_s[s, p] * incoming[s, part, :, 0:width].astype(F32)
        return (term - kmat) / denom

    def x_copy(c, r, d):
        return pltpu.make_async_remote_copy(
            src_ref=tx[c].at[r, d], dst_ref=rx[c].at[r, g],
            send_sem=x_send.at[r, c], recv_sem=x_recv.at[r, c],
            device_id=(a, lax.rem(g + d, n_grp)), device_id_type=MESH,
        )

    def exchange(c, r):
        c0, c1 = chunks[c]
        incoming = None if r == 0 else rx[c].at[r - 1]
        for d in list(range(1, n_grp)) + [0]:
            p = send_pair[0, lax.rem(g + d, n_grp)]
            for part in range(2 if c0 else 1):
                width = c0 if part else c1
                v = strip(c, p, part, incoming).astype(BF16)
                if d:
                    tx[c][r, d, part, :, 0:width] = v
                else:
                    rx[c][r, g, part, :, 0:width] = v
            if d:
                x_copy(c, r, d).start()

    def wait_exchange(c, r):
        ref = tx[c].at[r, pl.ds(1, n_grp - 1)]
        pltpu.make_async_copy(ref, ref, x_recv.at[r, c]).wait()

    def finish(c):
        c0, c1 = chunks[c]
        incoming = rx[c].at[ITERS - 1]

        @pl.loop(0, pairs, unroll=4)
        def _(p):
            out[p, c0:c1, 0:c1] = strip(c, p, 0, incoming)
            if c0:
                base = c0 // LANES * LANES
                top = max(c1, base + LANES)
                v = strip(c, p, 1, incoming)
                if c0 > base:
                    v = jnp.concatenate([jnp.zeros((c0 - base, c0), F32), v], axis=0)
                if c1 < top:
                    v = jnp.concatenate([v, jnp.zeros((top - c1, c0), F32)], axis=0)
                out[p, 0:c0, c0:c1] = jnp.transpose(v)[:, c0 - base:c1 - base]

    n = len(chunks)
    for t in range(n + ITERS):
        if t < n:
            wait_blocks(t)
            fit(t)
            gram(t)
            exchange(t, 0)
        for r in range(1, ITERS):
            if 0 <= t - r < n:
                wait_exchange(t - r, r - 1)
                exchange(t - r, r)
        if t + 2 < n:
            send_chunk(t + 2)
        if 0 <= t - ITERS < n:
            wait_exchange(t - ITERS, ITERS - 1)
            finish(t - ITERS)

    ref = idx_rx.at[pl.ds(1, n_aux - 1)]
    pltpu.make_async_copy(ref, ref, idx_send).wait()
    for c, (c0, c1) in enumerate(chunks):
        ref = pk.at[pl.ds(0, n_dev - 1), pl.ds(c0, c1 - c0), :]
        pltpu.make_async_copy(ref, ref, a_send.at[c]).wait()
        for r in range(ITERS):
            ref = tx[c].at[r, pl.ds(1, n_grp - 1)]
            pltpu.make_async_copy(ref, ref, x_send.at[r, c]).wait()


def fused(integrals, metric, fock, virt_energy, send_orb, pair_orb, send_pair, cpl_slot, cpl_orb):
    rows, group_orbs, nv = integrals.shape
    n_aux = lax.axis_size("aux")
    n_grp = lax.axis_size("grp")
    naux = n_aux * rows
    od = group_orbs // n_aux
    pairs = pair_orb.shape[0]
    chunks = chunks_of(nv)
    n = len(chunks)
    dims = (n_aux, n_grp, rows, od, nv, pairs, group_orbs, chunks)
    dma = pltpu.SemaphoreType.DMA
    hbm = pl.BlockSpec(memory_space=pltpu.HBM)
    vmem = pl.BlockSpec(memory_space=pltpu.VMEM)

    def here(x):
        return pltpu.with_memory_space_constraint(x, pltpu.HBM)

    small = [
        virt_energy[None, :], send_orb, pair_orb.T, send_pair,
        cpl_slot.T, jnp.transpose(cpl_orb, (1, 2, 0)),
    ]
    parts = [(2 if c0 else 1, c1 - c0, up(c1)) for c0, c1 in chunks]
    return pl.pallas_call(
        functools.partial(fused_kernel, dims),
        out_shape=pltpu.VMEM((pairs, nv, nv), F32),
        in_specs=[hbm] * 9,
        out_specs=vmem,
        scratch_shapes=[
            pltpu.VMEM((n_aux, rows, od, nv), BF16),
            pltpu.VMEM((n_aux * n_grp, nv, rows), BF16),
            pltpu.VMEM((n_grp, nv, naux), BF16),
            pltpu.VMEM((n_grp, nv, naux), BF16),
            pltpu.VMEM(metric.shape, BF16),
            pltpu.VMEM(metric.shape, BF16),
            pltpu.VMEM(fock.shape, BF16),
            pltpu.VMEM((nv, nv), F32),
            pltpu.VMEM((8, LANES), jnp.int32),
            pltpu.VMEM((n_aux, 8, LANES), jnp.int32),
            pltpu.VMEM((8, LANES), F32),
            pltpu.SMEM((8, LANES), F32),
            pltpu.VMEM((1, nv), F32),
            pltpu.SMEM(send_orb.shape, jnp.int32),
            pltpu.SMEM((2, pairs), jnp.int32),
            pltpu.VMEM((2, pairs), jnp.int32),
            pltpu.SMEM(send_pair.shape, jnp.int32),
            pltpu.VMEM(small[4].shape, jnp.int32),
            pltpu.VMEM(small[5].shape, jnp.int32),
            [pltpu.VMEM((n_grp * n_grp, c1 - c0, up(c1)), F32) for c0, c1 in chunks],
            [pltpu.VMEM((ITERS, n_grp, *p), BF16) for p in parts],
            [pltpu.VMEM((ITERS, n_grp, *p), BF16) for p in parts],
            dma((n_aux,)), dma, dma, dma, dma((7,)), dma, dma, dma((n,)),
            dma((n,)), dma((n,)), dma((ITERS, n)), dma((ITERS, n)),
        ],
        compiler_params=pltpu.CompilerParams(
            collective_id=0, has_side_effects=True, vmem_limit_bytes=52 * 1024 * 1024
        ),
    )(*[here(x) for x in [integrals, metric, fock] + small])


def fits_fused(integrals, pair_orb):
    rows, group_orbs, nv = integrals.shape
    n_aux, n_grp = lax.axis_size("aux"), lax.axis_size("grp")
    return (
        rows % LANES == 0
        and nv % (2 * LANES) == 0
        and n_aux % 2 == 0
        and group_orbs == 16 * n_aux
        and n_grp < 8
        and n_grp * n_grp <= pair_orb.shape[0] <= LANES
    )


def final_kernel(idx_i, idx_j, mixing, diag, fit_ref, ve_col, ve_row, inc_ref, out_ref):
    p = pl.program_id(0)
    kmat = lax.dot_general(
        fit_ref[idx_i[p]],
        fit_ref[idx_j[p]],
        (((0,), (0,)), ((), ())),
        preferred_element_type=jnp.float32,
    )
    term = mixing[p, 0] * inc_ref[0].astype(jnp.float32)
    for s in range(1, inc_ref.shape[0]):
        term = term + mixing[p, s] * inc_ref[s].astype(jnp.float32)
    denom = (ve_col[...] + ve_row[...]) - diag[p]
    out_ref[0] = (term - kmat) / denom


def final_call(idx_i, idx_j, mixing, diag, fitted, virt_energy, incoming):
    pairs = idx_i.shape[0]
    nv = virt_energy.shape[0]
    whole = pl.BlockSpec(memory_space=pltpu.VMEM)
    return pl.pallas_call(
        final_kernel,
        out_shape=jax.ShapeDtypeStruct((pairs, nv, nv), jnp.float32),
        grid_spec=pltpu.PrefetchScalarGridSpec(
            num_scalar_prefetch=4,
            grid=(pairs,),
            in_specs=[whole, whole, whole, whole],
            out_specs=pl.BlockSpec((1, nv, nv), lambda p, *_: (p, 0, 0)),
        ),
    )(idx_i, idx_j, mixing, diag, fitted, virt_energy[:, None], virt_energy[None, :], incoming)


def stepwise(
    integrals, metric, fock, virt_energy, send_orb, pair_orb, send_pair, cpl_slot, cpl_orb
):
    rows, group_orbs, nv = integrals.shape
    n_aux = lax.axis_size("aux")
    n_grp = lax.axis_size("grp")
    orb_dev = group_orbs // n_aux
    spread = jnp.broadcast_to(send_orb, (n_aux, n_grp))
    wanted = lax.all_to_all(spread, "aux", split_axis=0, concat_axis=0, tiled=True)
    idx = (jnp.arange(n_aux, dtype=jnp.int32)[:, None] * orb_dev + wanted).reshape(-1)
    packed = jnp.transpose(jnp.take(integrals, idx, axis=1, mode="clip"), (1, 0, 2))
    block = lax.all_to_all(packed, ("aux", "grp"), split_axis=0, concat_axis=0, tiled=True)
    block = block.reshape(n_aux, n_grp, rows, nv)
    block = jnp.transpose(block, (0, 2, 1, 3)).reshape(n_aux * rows, n_grp * nv)
    fitted = jnp.dot(metric, block, preferred_element_type=jnp.float32).astype(jnp.bfloat16)
    fitted = jnp.transpose(fitted.reshape(n_aux * rows, n_grp, nv), (1, 0, 2))

    orb_i = pair_orb[:, 0]
    orb_j = pair_orb[:, 1]
    idx_i = orb_i // group_orbs
    idx_j = orb_j // group_orbs
    diag_sum = fock[orb_i, orb_i].astype(jnp.float32) + fock[orb_j, orb_j].astype(jnp.float32)
    k_orb = cpl_orb[:, :, 0]
    l_orb = cpl_orb[:, :, 1]
    first = (l_orb == orb_j[:, None]) & (k_orb != orb_i[:, None])
    second = (k_orb == orb_i[:, None]) & (l_orb != orb_j[:, None])
    f_ik = fock[orb_i[:, None], k_orb].astype(jnp.float32)
    f_jl = fock[orb_j[:, None], l_orb].astype(jnp.float32)
    weight = jnp.where(first, f_ik, 0.0) + jnp.where(second, f_jl, 0.0)
    onehot = cpl_slot[:, :, None] == jnp.arange(n_grp, dtype=jnp.int32)[None, None, :]
    mixing = jnp.sum(jnp.where(onehot, weight[:, :, None], 0.0), axis=1)

    sent = send_pair[0]
    zeros = jnp.zeros((n_grp, nv, nv), jnp.bfloat16)
    s_i, s_j, s_mix, s_diag = idx_i[sent], idx_j[sent], mixing[sent], diag_sum[sent]
    incoming = zeros
    for step in range(ITERS):
        amps = final_call(s_i, s_j, s_mix, s_diag, fitted, virt_energy, incoming)
        incoming = lax.all_to_all(
            amps.astype(jnp.bfloat16), "grp", split_axis=0, concat_axis=0, tiled=True
        )
    return final_call(idx_i, idx_j, mixing, diag_sum, fitted, virt_energy, incoming)


def on_device(*args):
    return fused(*args) if fits_fused(args[0], args[5]) else stepwise(*args)


def solution(mesh):
    in_specs = (
        P("aux", "grp", None),
        P(),
        P(),
        P(),
        P(("aux", "grp"), None),
        P(("aux", "grp"), None),
        P(("aux", "grp"), None),
        P(("aux", "grp"), None),
        P(("aux", "grp"), None, None),
    )
    out_specs = P(("aux", "grp"), None, None)
    return jax.shard_map(
        on_device, mesh=mesh, in_specs=in_specs, out_specs=out_specs, check_vma=False
    )
```

```python
import functools

import jax
import jax.numpy as jnp
from jax import lax
from jax.experimental import pallas as pl
from jax.experimental.pallas import tpu as pltpu
from jax.sharding import PartitionSpec as P

ITERS = 2
MESH = pl.DeviceIdType.MESH
F32 = jnp.float32
BF16 = jnp.bfloat16
NT = (((1,), (1,)), ((), ()))
LANES = 128


def chunks_of(nv):
    cuts = [0, nv // 2, nv * 3 // 4, nv * 7 // 8, nv]
    return list(zip(cuts[:-1], cuts[1:]))


def up(n):
    return -(-n // LANES) * LANES


def fused_kernel(
    dims,
    integrals, metric, fock, ve_hbm, orb_hbm, pair_hbm, mine_hbm, slot_hbm, cpl_hbm,
    out,
    raw, pk, it, ft, met, met_t, fk, vsum, idx_tx, idx_rx, wt_v, wt_s,
    ve_row, send_orb, pair_s, pair_v, send_pair, slot_v, cpl_v,
    gs, tx, rx,
    raw_sem, met_sem, fk_sem, wt_sem, small_sem, idx_send, idx_recv, own_sem,
    a_send, a_recv, x_send, x_recv, here_sem,
):
    n_aux, n_grp, rows, od, nv, pairs, group_orbs, chunks = dims
    a = lax.axis_index("aux")
    g = lax.axis_index("grp")
    n_dev = n_aux * n_grp
    half = n_aux // 2

    def col_of(k):
        off = half + jnp.where(k % 2 == 0, k // 2, -((k + 1) // 2))
        return lax.rem(a + off, n_aux)

    def raw_copy(k, col):
        first = pl.multiple_of(col * od, od)
        return pltpu.make_async_copy(integrals.at[:, pl.ds(first, od), :], raw.at[k], raw_sem.at[k])

    small = [
        pltpu.make_async_copy(src, dst, small_sem.at[k])
        for k, (src, dst) in enumerate([
            (orb_hbm, send_orb), (mine_hbm, send_pair), (pair_hbm, pair_s), (pair_hbm, pair_v),
            (slot_hbm, slot_v), (cpl_hbm, cpl_v), (ve_hbm, ve_row),
        ])
    ]
    for copy in small:
        copy.start()
    barrier = pltpu.get_barrier_semaphore()

    row_peers = [(lax.rem(a + k, n_aux), g) for k in range(1, n_aux)]
    grp_peers = [(a, lax.rem(g + k, n_grp)) for k in range(1, n_grp)]
    for peer in row_peers + grp_peers:
        pl.semaphore_signal(barrier, inc=1, device_id=peer, device_id_type=MESH)

    @pl.loop(0, n_aux)
    def _(k):
        raw_copy(k, col_of(k)).start()

    met_copy = pltpu.make_async_copy(metric, met, met_sem)
    fk_copy = pltpu.make_async_copy(fock, fk, fk_sem)
    met_copy.start()
    fk_copy.start()
    small[0].wait()
    for s in range(n_grp):
        idx_tx[pl.ds(s, 1), :] = jnp.full((1, LANES), send_orb[0, s], jnp.int32)
        idx_rx[a, pl.ds(s, 1), :] = jnp.full((1, LANES), send_orb[0, s], jnp.int32)

    pl.semaphore_wait(barrier, n_aux - 1 + n_grp - 1)

    def idx_copy(k):
        t = lax.rem(a + k, n_aux)
        return pltpu.make_async_remote_copy(
            src_ref=idx_tx, dst_ref=idx_rx.at[a], send_sem=idx_send, recv_sem=idx_recv,
            device_id=(t, g), device_id_type=MESH,
        )

    @pl.loop(1, n_aux)
    def _(k):
        idx_copy(k).start()

    for peer in grp_peers:
        pl.semaphore_signal(here_sem, inc=1, device_id=peer, device_id_type=MESH)

    idx_all = pltpu.make_async_copy(idx_rx.at[pl.ds(1, n_aux - 1)], idx_rx.at[pl.ds(1, n_aux - 1)], idx_recv)
    idx_all.wait()
    pl.semaphore_wait(here_sem, n_grp - 1)

    def block_copy(c, col, grp):
        c0, c1 = chunks[c]
        lane0 = pl.multiple_of(a * rows, rows)
        return pltpu.make_async_remote_copy(
            src_ref=pk.at[col * n_grp + grp, pl.ds(c0, c1 - c0), :],
            dst_ref=it.at[g, pl.ds(c0, c1 - c0), pl.ds(lane0, rows)],
            send_sem=a_send.at[c], recv_sem=a_recv.at[c],
            device_id=(col, grp), device_id_type=MESH,
        )

    def own_copy(c):
        c0, c1 = chunks[c]
        lane0 = pl.multiple_of(a * rows, rows)
        return pltpu.make_async_copy(
            pk.at[a * n_grp + g, pl.ds(c0, c1 - c0), :],
            it.at[g, pl.ds(c0, c1 - c0), pl.ds(lane0, rows)],
            own_sem.at[c],
        )

    def send_far(c, k):
        col = col_of(k)
        for d in range(n_grp):
            block_copy(c, col, lax.rem(g + d, n_grp)).start()

    def send_own(c):
        for d in range(1, n_grp):
            block_copy(c, a, lax.rem(g + d, n_grp)).start()
        own_copy(c).start()

    step = 2 * LANES // od
    lane = lax.broadcasted_iota(jnp.int32, (step, 2 * LANES), 1)
    row = lax.broadcasted_iota(jnp.int32, (step, 2 * LANES), 0)

    def select(k, col):
        raw_copy(k, col).wait()
        pick = []
        for s in range(n_grp):
            v = idx_rx[col, pl.ds(s, 1), :]
            v = jnp.broadcast_to(jnp.concatenate([v, v], axis=1), (step, 2 * LANES))
            pick.append(jnp.where(lane == row * od + v, 1.0, 0.0))
        sel = jnp.concatenate(pick, axis=0).astype(BF16)
        parts = []
        for t in range(rows // step):
            x = raw[k, t * step:(t + 1) * step].reshape(step * od, nv)
            parts.append(jnp.dot(sel, x, preferred_element_type=F32))
        for s in range(n_grp):
            blk = jnp.concatenate([p[s * step:(s + 1) * step] for p in parts], axis=0)
            pk[col * n_grp + s] = jnp.transpose(blk).astype(BF16)

    @pl.loop(0, n_aux - 1)
    def _(k):
        select(k, col_of(k))
        send_far(0, k)

    select(n_aux - 1, a)
    send_own(0)

    def send_chunk(c):
        @pl.loop(0, n_aux - 1)
        def _(k):
            send_far(c, k)

        send_own(c)

    send_chunk(1)

    for copy in small[1:]:
        copy.wait()
    ve = ve_row[...]
    vb = jnp.broadcast_to(ve, (nv, nv))
    vsum[...] = jnp.transpose(vb) + vb

    fk_copy.wait()
    orb_i = pair_v[pl.ds(0, 1), :]
    orb_j = pair_v[pl.ds(1, 1), :]
    nocc = fk.shape[0]
    orbs = lax.broadcasted_iota(jnp.int32, (nocc, pairs), 0)
    at_i = orbs == orb_i
    at_j = orbs == orb_j
    tn = (((0,), (0,)), ((), ()))
    f_i = lax.dot_general(fk[...], jnp.where(at_i, 1.0, 0.0).astype(BF16), tn, preferred_element_type=F32)
    f_j = lax.dot_general(fk[...], jnp.where(at_j, 1.0, 0.0).astype(BF16), tn, preferred_element_type=F32)

    def entry(mask, table):
        return jnp.sum(jnp.where(mask, table, 0.0), axis=0, keepdims=True)

    pad = jnp.zeros((1, LANES - pairs), F32)
    mix = [jnp.zeros((1, pairs), F32) for _ in range(n_grp)]
    for e in range(cpl_v.shape[0]):
        k_orb = cpl_v[e, pl.ds(0, 1), :]
        l_orb = cpl_v[e, pl.ds(1, 1), :]
        f_ik = entry(orbs == k_orb, f_i)
        f_jl = entry(orbs == l_orb, f_j)
        w = jnp.where((l_orb == orb_j) & (k_orb != orb_i), f_ik, 0.0)
        w = w + jnp.where((k_orb == orb_i) & (l_orb != orb_j), f_jl, 0.0)
        slot = slot_v[pl.ds(e, 1), :]
        for s in range(n_grp):
            mix[s] = mix[s] + jnp.where(slot == s, w, 0.0)
    diag = entry(at_i, f_i) + entry(at_j, f_j)
    for s in range(n_grp):
        wt_v[pl.ds(s, 1), :] = jnp.concatenate([mix[s], pad], axis=1)
    wt_v[pl.ds(n_grp, 1), :] = jnp.concatenate([diag, pad], axis=1)
    wt_copy = pltpu.make_async_copy(wt_v, wt_s, wt_sem)
    wt_copy.start()
    wt_copy.wait()
    met_copy.wait()
    side = 2 * LANES

    @pl.loop(0, met.shape[0] // side)
    def _(t):
        q0 = pl.multiple_of(t * side, side)
        for r in range(0, met.shape[1], side):
            met_t[r:r + side, pl.ds(q0, side)] = jnp.transpose(met[pl.ds(q0, side), r:r + side])

    def wait_blocks(c):
        c0, c1 = chunks[c]
        ref = pk.at[pl.ds(0, n_dev - 1), pl.ds(c0, c1 - c0), :]
        own_copy(c).wait()
        pltpu.make_async_copy(ref, ref, a_recv.at[c]).wait()

    def fit(c):
        c0, c1 = chunks[c]
        w = c1 - c0
        left = it[:, c0:c1, :].reshape(n_grp * w, n_aux * rows)
        for q0 in range(0, n_aux * rows, side):
            f = jnp.dot(left, met_t[:, q0:q0 + side], preferred_element_type=F32)
            ft[:, pl.ds(c0, w), pl.ds(q0, side)] = f.astype(BF16).reshape(n_grp, w, side)

    def gram(c):
        c0, c1 = chunks[c]
        w = c1 - c0
        left = ft[:, c0:c1, :].reshape(n_grp * w, n_aux * rows)

        for o in range(n_grp):
            k = lax.dot_general(left, ft[o, 0:c1, :], NT, preferred_element_type=F32)
            for s in range(n_grp):
                gs[c][s * n_grp + o, :, 0:c1] = k[s * w:(s + 1) * w]

    def slots(p):
        return pair_s[0, p] // group_orbs, pair_s[1, p] // group_orbs

    def strip(c, p, part, incoming):
        c0, c1 = chunks[c]
        width = c0 if part else c1
        i, j = slots(p)
        which = j * n_grp + i if part else i * n_grp + j
        kmat = gs[c][which, :, 0:width]
        denom = vsum[c0:c1, 0:width] - wt_s[n_grp, p]
        if incoming is None:
            return -(kmat / denom)
        term = wt_s[0, p] * incoming[0, part, :, 0:width].astype(F32)
        for s in range(1, n_grp):
            term = term + wt_s[s, p] * incoming[s, part, :, 0:width].astype(F32)
        return (term - kmat) / denom

    def x_copy(c, r, d):
        return pltpu.make_async_remote_copy(
            src_ref=tx[c].at[r, d], dst_ref=rx[c].at[r, g],
            send_sem=x_send.at[r, c], recv_sem=x_recv.at[r, c],
            device_id=(a, lax.rem(g + d, n_grp)), device_id_type=MESH,
        )

    def exchange(c, r):
        c0, c1 = chunks[c]
        incoming = None if r == 0 else rx[c].at[r - 1]
        for d in list(range(1, n_grp)) + [0]:
            p = send_pair[0, lax.rem(g + d, n_grp)]
            for part in range(2 if c0 else 1):
                width = c0 if part else c1
                v = strip(c, p, part, incoming).astype(BF16)
                if d:
                    tx[c][r, d, part, :, 0:width] = v
                else:
                    rx[c][r, g, part, :, 0:width] = v
            if d:
                x_copy(c, r, d).start()

    def wait_exchange(c, r):
        ref = tx[c].at[r, pl.ds(1, n_grp - 1)]
        pltpu.make_async_copy(ref, ref, x_recv.at[r, c]).wait()

    def finish(c):
        c0, c1 = chunks[c]
        incoming = rx[c].at[ITERS - 1]

        @pl.loop(0, pairs, unroll=4)
        def _(p):
            out[p, c0:c1, 0:c1] = strip(c, p, 0, incoming)
            if c0:
                base = c0 // LANES * LANES
                top = max(c1, base + LANES)
                v = strip(c, p, 1, incoming)
                if c0 > base:
                    v = jnp.concatenate([jnp.zeros((c0 - base, c0), F32), v], axis=0)
                if c1 < top:
                    v = jnp.concatenate([v, jnp.zeros((top - c1, c0), F32)], axis=0)
                out[p, 0:c0, c0:c1] = jnp.transpose(v)[:, c0 - base:c1 - base]

    n = len(chunks)
    for t in range(n + ITERS):
        if t < n:
            wait_blocks(t)
            fit(t)
            gram(t)
            exchange(t, 0)
        for r in range(1, ITERS):
            if 0 <= t - r < n:
                wait_exchange(t - r, r - 1)
                exchange(t - r, r)
        if t + 2 < n:
            send_chunk(t + 2)
        if 0 <= t - ITERS < n:
            wait_exchange(t - ITERS, ITERS - 1)
            finish(t - ITERS)

    ref = idx_rx.at[pl.ds(1, n_aux - 1)]
    pltpu.make_async_copy(ref, ref, idx_send).wait()
    for c, (c0, c1) in enumerate(chunks):
        ref = pk.at[pl.ds(0, n_dev - 1), pl.ds(c0, c1 - c0), :]
        pltpu.make_async_copy(ref, ref, a_send.at[c]).wait()
        for r in range(ITERS):
            ref = tx[c].at[r, pl.ds(1, n_grp - 1)]
            pltpu.make_async_copy(ref, ref, x_send.at[r, c]).wait()


def fused(integrals, metric, fock, virt_energy, send_orb, pair_orb, send_pair, cpl_slot, cpl_orb):
    rows, group_orbs, nv = integrals.shape
    n_aux = lax.axis_size("aux")
    n_grp = lax.axis_size("grp")
    naux = n_aux * rows
    od = group_orbs // n_aux
    pairs = pair_orb.shape[0]
    chunks = chunks_of(nv)
    n = len(chunks)
    dims = (n_aux, n_grp, rows, od, nv, pairs, group_orbs, chunks)
    dma = pltpu.SemaphoreType.DMA
    hbm = pl.BlockSpec(memory_space=pltpu.HBM)
    vmem = pl.BlockSpec(memory_space=pltpu.VMEM)

    def here(x):
        return pltpu.with_memory_space_constraint(x, pltpu.HBM)

    small = [
        virt_energy[None, :], send_orb, pair_orb.T, send_pair,
        cpl_slot.T, jnp.transpose(cpl_orb, (1, 2, 0)),
    ]
    parts = [(2 if c0 else 1, c1 - c0, up(c1)) for c0, c1 in chunks]
    return pl.pallas_call(
        functools.partial(fused_kernel, dims),
        out_shape=pltpu.VMEM((pairs, nv, nv), F32),
        in_specs=[hbm] * 9,
        out_specs=vmem,
        scratch_shapes=[
            pltpu.VMEM((n_aux, rows, od, nv), BF16),
            pltpu.VMEM((n_aux * n_grp, nv, rows), BF16),
            pltpu.VMEM((n_grp, nv, naux), BF16),
            pltpu.VMEM((n_grp, nv, naux), BF16),
            pltpu.VMEM(metric.shape, BF16),
            pltpu.VMEM(metric.shape, BF16),
            pltpu.VMEM(fock.shape, BF16),
            pltpu.VMEM((nv, nv), F32),
            pltpu.VMEM((8, LANES), jnp.int32),
            pltpu.VMEM((n_aux, 8, LANES), jnp.int32),
            pltpu.VMEM((8, LANES), F32),
            pltpu.SMEM((8, LANES), F32),
            pltpu.VMEM((1, nv), F32),
            pltpu.SMEM(send_orb.shape, jnp.int32),
            pltpu.SMEM((2, pairs), jnp.int32),
            pltpu.VMEM((2, pairs), jnp.int32),
            pltpu.SMEM(send_pair.shape, jnp.int32),
            pltpu.VMEM(small[4].shape, jnp.int32),
            pltpu.VMEM(small[5].shape, jnp.int32),
            [pltpu.VMEM((n_grp * n_grp, c1 - c0, up(c1)), F32) for c0, c1 in chunks],
            [pltpu.VMEM((ITERS, n_grp, *p), BF16) for p in parts],
            [pltpu.VMEM((ITERS, n_grp, *p), BF16) for p in parts],
            dma((n_aux,)), dma, dma, dma, dma((7,)), dma, dma, dma((n,)),
            dma((n,)), dma((n,)), dma((ITERS, n)), dma((ITERS, n)), pltpu.SemaphoreType.REGULAR,
        ],
        compiler_params=pltpu.CompilerParams(
            collective_id=0, has_side_effects=True, vmem_limit_bytes=52 * 1024 * 1024
        ),
    )(*[here(x) for x in [integrals, metric, fock] + small])


def fits_fused(integrals, pair_orb):
    rows, group_orbs, nv = integrals.shape
    n_aux, n_grp = lax.axis_size("aux"), lax.axis_size("grp")
    return (
        rows % LANES == 0
        and nv % (2 * LANES) == 0
        and n_aux % 2 == 0
        and group_orbs == 16 * n_aux
        and n_grp < 8
        and n_grp * n_grp <= pair_orb.shape[0] <= LANES
    )


def final_kernel(idx_i, idx_j, mixing, diag, fit_ref, ve_col, ve_row, inc_ref, out_ref):
    p = pl.program_id(0)
    kmat = lax.dot_general(
        fit_ref[idx_i[p]],
        fit_ref[idx_j[p]],
        (((0,), (0,)), ((), ())),
        preferred_element_type=jnp.float32,
    )
    term = mixing[p, 0] * inc_ref[0].astype(jnp.float32)
    for s in range(1, inc_ref.shape[0]):
        term = term + mixing[p, s] * inc_ref[s].astype(jnp.float32)
    denom = (ve_col[...] + ve_row[...]) - diag[p]
    out_ref[0] = (term - kmat) / denom


def final_call(idx_i, idx_j, mixing, diag, fitted, virt_energy, incoming):
    pairs = idx_i.shape[0]
    nv = virt_energy.shape[0]
    whole = pl.BlockSpec(memory_space=pltpu.VMEM)
    return pl.pallas_call(
        final_kernel,
        out_shape=jax.ShapeDtypeStruct((pairs, nv, nv), jnp.float32),
        grid_spec=pltpu.PrefetchScalarGridSpec(
            num_scalar_prefetch=4,
            grid=(pairs,),
            in_specs=[whole, whole, whole, whole],
            out_specs=pl.BlockSpec((1, nv, nv), lambda p, *_: (p, 0, 0)),
        ),
    )(idx_i, idx_j, mixing, diag, fitted, virt_energy[:, None], virt_energy[None, :], incoming)


def stepwise(
    integrals, metric, fock, virt_energy, send_orb, pair_orb, send_pair, cpl_slot, cpl_orb
):
    rows, group_orbs, nv = integrals.shape
    n_aux = lax.axis_size("aux")
    n_grp = lax.axis_size("grp")
    orb_dev = group_orbs // n_aux
    spread = jnp.broadcast_to(send_orb, (n_aux, n_grp))
    wanted = lax.all_to_all(spread, "aux", split_axis=0, concat_axis=0, tiled=True)
    idx = (jnp.arange(n_aux, dtype=jnp.int32)[:, None] * orb_dev + wanted).reshape(-1)
    packed = jnp.transpose(jnp.take(integrals, idx, axis=1, mode="clip"), (1, 0, 2))
    block = lax.all_to_all(packed, ("aux", "grp"), split_axis=0, concat_axis=0, tiled=True)
    block = block.reshape(n_aux, n_grp, rows, nv)
    block = jnp.transpose(block, (0, 2, 1, 3)).reshape(n_aux * rows, n_grp * nv)
    fitted = jnp.dot(metric, block, preferred_element_type=jnp.float32).astype(jnp.bfloat16)
    fitted = jnp.transpose(fitted.reshape(n_aux * rows, n_grp, nv), (1, 0, 2))

    orb_i = pair_orb[:, 0]
    orb_j = pair_orb[:, 1]
    idx_i = orb_i // group_orbs
    idx_j = orb_j // group_orbs
    diag_sum = fock[orb_i, orb_i].astype(jnp.float32) + fock[orb_j, orb_j].astype(jnp.float32)
    k_orb = cpl_orb[:, :, 0]
    l_orb = cpl_orb[:, :, 1]
    first = (l_orb == orb_j[:, None]) & (k_orb != orb_i[:, None])
    second = (k_orb == orb_i[:, None]) & (l_orb != orb_j[:, None])
    f_ik = fock[orb_i[:, None], k_orb].astype(jnp.float32)
    f_jl = fock[orb_j[:, None], l_orb].astype(jnp.float32)
    weight = jnp.where(first, f_ik, 0.0) + jnp.where(second, f_jl, 0.0)
    onehot = cpl_slot[:, :, None] == jnp.arange(n_grp, dtype=jnp.int32)[None, None, :]
    mixing = jnp.sum(jnp.where(onehot, weight[:, :, None], 0.0), axis=1)

    sent = send_pair[0]
    zeros = jnp.zeros((n_grp, nv, nv), jnp.bfloat16)
    s_i, s_j, s_mix, s_diag = idx_i[sent], idx_j[sent], mixing[sent], diag_sum[sent]
    incoming = zeros
    for step in range(ITERS):
        amps = final_call(s_i, s_j, s_mix, s_diag, fitted, virt_energy, incoming)
        incoming = lax.all_to_all(
            amps.astype(jnp.bfloat16), "grp", split_axis=0, concat_axis=0, tiled=True
        )
    return final_call(idx_i, idx_j, mixing, diag_sum, fitted, virt_energy, incoming)


def on_device(*args):
    return fused(*args) if fits_fused(args[0], args[5]) else stepwise(*args)


def solution(mesh):
    in_specs = (
        P("aux", "grp", None),
        P(),
        P(),
        P(),
        P(("aux", "grp"), None),
        P(("aux", "grp"), None),
        P(("aux", "grp"), None),
        P(("aux", "grp"), None),
        P(("aux", "grp"), None, None),
    )
    out_specs = P(("aux", "grp"), None, None)
    return jax.shard_map(
        on_device, mesh=mesh, in_specs=in_specs, out_specs=out_specs, check_vma=False
    )
```

```python
import functools

import jax
import jax.numpy as jnp
from jax import lax
from jax.experimental import pallas as pl
from jax.experimental.pallas import tpu as pltpu
from jax.sharding import PartitionSpec as P

ITERS = 2
MESH = pl.DeviceIdType.MESH
F32 = jnp.float32
BF16 = jnp.bfloat16
NT = (((1,), (1,)), ((), ()))
LANES = 128


def chunks_of(nv):
    cuts = [0, nv // 2, nv * 3 // 4, nv * 7 // 8, nv]
    return list(zip(cuts[:-1], cuts[1:]))


def up(n):
    return -(-n // LANES) * LANES


def fused_kernel(
    dims,
    integrals, metric, fock, ve_hbm, orb_hbm, pair_hbm, mine_hbm, slot_hbm, cpl_hbm,
    out, k_last, x_last, wt_last, v_last,
    raw, pk, it, ft, met, met_t, fk, vsum, idx_tx, idx_rx, wt_v, wt_s,
    ve_row, send_orb, pair_s, pair_v, send_pair, slot_v, cpl_v,
    gs, tx, rx,
    raw_sem, met_sem, fk_sem, wt_sem, small_sem, idx_send, idx_recv, own_sem,
    a_send, a_recv, x_send, x_recv, here_sem,
):
    n_aux, n_grp, rows, od, nv, pairs, group_orbs, chunks = dims
    a = lax.axis_index("aux")
    g = lax.axis_index("grp")
    n_dev = n_aux * n_grp
    half = n_aux // 2

    def col_of(k):
        off = half + jnp.where(k % 2 == 0, k // 2, -((k + 1) // 2))
        return lax.rem(a + off, n_aux)

    def raw_copy(k, col):
        first = pl.multiple_of(col * od, od)
        return pltpu.make_async_copy(integrals.at[:, pl.ds(first, od), :], raw.at[k], raw_sem.at[k])

    small = [
        pltpu.make_async_copy(src, dst, small_sem.at[k])
        for k, (src, dst) in enumerate([
            (orb_hbm, send_orb), (mine_hbm, send_pair), (pair_hbm, pair_s), (pair_hbm, pair_v),
            (slot_hbm, slot_v), (cpl_hbm, cpl_v), (ve_hbm, ve_row),
        ])
    ]
    for copy in small:
        copy.start()
    barrier = pltpu.get_barrier_semaphore()

    row_peers = [(lax.rem(a + k, n_aux), g) for k in range(1, n_aux)]
    grp_peers = [(a, lax.rem(g + k, n_grp)) for k in range(1, n_grp)]
    for peer in row_peers + grp_peers:
        pl.semaphore_signal(barrier, inc=1, device_id=peer, device_id_type=MESH)

    @pl.loop(0, n_aux)
    def _(k):
        raw_copy(k, col_of(k)).start()

    met_copy = pltpu.make_async_copy(metric, met, met_sem)
    fk_copy = pltpu.make_async_copy(fock, fk, fk_sem)
    met_copy.start()
    fk_copy.start()
    small[0].wait()
    for s in range(n_grp):
        idx_tx[pl.ds(s, 1), :] = jnp.full((1, LANES), send_orb[0, s], jnp.int32)
        idx_rx[a, pl.ds(s, 1), :] = jnp.full((1, LANES), send_orb[0, s], jnp.int32)

    pl.semaphore_wait(barrier, n_aux - 1 + n_grp - 1)

    def idx_copy(k):
        t = lax.rem(a + k, n_aux)
        return pltpu.make_async_remote_copy(
            src_ref=idx_tx, dst_ref=idx_rx.at[a], send_sem=idx_send, recv_sem=idx_recv,
            device_id=(t, g), device_id_type=MESH,
        )

    @pl.loop(1, n_aux)
    def _(k):
        idx_copy(k).start()

    for peer in grp_peers:
        pl.semaphore_signal(here_sem, inc=1, device_id=peer, device_id_type=MESH)

    idx_all = pltpu.make_async_copy(idx_rx.at[pl.ds(1, n_aux - 1)], idx_rx.at[pl.ds(1, n_aux - 1)], idx_recv)
    idx_all.wait()
    pl.semaphore_wait(here_sem, n_grp - 1)

    def block_copy(c, col, grp):
        c0, c1 = chunks[c]
        lane0 = pl.multiple_of(a * rows, rows)
        return pltpu.make_async_remote_copy(
            src_ref=pk.at[col * n_grp + grp, pl.ds(c0, c1 - c0), :],
            dst_ref=it.at[g, pl.ds(c0, c1 - c0), pl.ds(lane0, rows)],
            send_sem=a_send.at[c], recv_sem=a_recv.at[c],
            device_id=(col, grp), device_id_type=MESH,
        )

    def own_copy(c):
        c0, c1 = chunks[c]
        lane0 = pl.multiple_of(a * rows, rows)
        return pltpu.make_async_copy(
            pk.at[a * n_grp + g, pl.ds(c0, c1 - c0), :],
            it.at[g, pl.ds(c0, c1 - c0), pl.ds(lane0, rows)],
            own_sem.at[c],
        )

    def send_far(c, k):
        col = col_of(k)
        for d in range(n_grp):
            block_copy(c, col, lax.rem(g + d, n_grp)).start()

    def send_own(c):
        for d in range(1, n_grp):
            block_copy(c, a, lax.rem(g + d, n_grp)).start()
        own_copy(c).start()

    step = 2 * LANES // od
    lane = lax.broadcasted_iota(jnp.int32, (step, 2 * LANES), 1)
    row = lax.broadcasted_iota(jnp.int32, (step, 2 * LANES), 0)

    def select(k, col):
        raw_copy(k, col).wait()
        pick = []
        for s in range(n_grp):
            v = idx_rx[col, pl.ds(s, 1), :]
            v = jnp.broadcast_to(jnp.concatenate([v, v], axis=1), (step, 2 * LANES))
            pick.append(jnp.where(lane == row * od + v, 1.0, 0.0))
        sel = jnp.concatenate(pick, axis=0).astype(BF16)
        parts = []
        for t in range(rows // step):
            x = raw[k, t * step:(t + 1) * step].reshape(step * od, nv)
            parts.append(jnp.dot(sel, x, preferred_element_type=F32))
        for s in range(n_grp):
            blk = jnp.concatenate([p[s * step:(s + 1) * step] for p in parts], axis=0)
            pk[col * n_grp + s] = jnp.transpose(blk).astype(BF16)

    @pl.loop(0, n_aux - 1)
    def _(k):
        select(k, col_of(k))
        send_far(0, k)

    select(n_aux - 1, a)
    send_own(0)

    def send_chunk(c):
        @pl.loop(0, n_aux - 1)
        def _(k):
            send_far(c, k)

        send_own(c)

    send_chunk(1)

    for copy in small[1:]:
        copy.wait()
    ve = ve_row[...]
    vb = jnp.broadcast_to(ve, (nv, nv))
    vsum[...] = jnp.transpose(vb) + vb

    fk_copy.wait()
    orb_i = pair_v[pl.ds(0, 1), :]
    orb_j = pair_v[pl.ds(1, 1), :]
    nocc = fk.shape[0]
    orbs = lax.broadcasted_iota(jnp.int32, (nocc, pairs), 0)
    at_i = orbs == orb_i
    at_j = orbs == orb_j
    tn = (((0,), (0,)), ((), ()))
    f_i = lax.dot_general(fk[...], jnp.where(at_i, 1.0, 0.0).astype(BF16), tn, preferred_element_type=F32)
    f_j = lax.dot_general(fk[...], jnp.where(at_j, 1.0, 0.0).astype(BF16), tn, preferred_element_type=F32)

    def entry(mask, table):
        return jnp.sum(jnp.where(mask, table, 0.0), axis=0, keepdims=True)

    pad = jnp.zeros((1, LANES - pairs), F32)
    mix = [jnp.zeros((1, pairs), F32) for _ in range(n_grp)]
    for e in range(cpl_v.shape[0]):
        k_orb = cpl_v[e, pl.ds(0, 1), :]
        l_orb = cpl_v[e, pl.ds(1, 1), :]
        f_ik = entry(orbs == k_orb, f_i)
        f_jl = entry(orbs == l_orb, f_j)
        w = jnp.where((l_orb == orb_j) & (k_orb != orb_i), f_ik, 0.0)
        w = w + jnp.where((k_orb == orb_i) & (l_orb != orb_j), f_jl, 0.0)
        slot = slot_v[pl.ds(e, 1), :]
        for s in range(n_grp):
            mix[s] = mix[s] + jnp.where(slot == s, w, 0.0)
    diag = entry(at_i, f_i) + entry(at_j, f_j)
    for s in range(n_grp):
        wt_v[pl.ds(s, 1), :] = jnp.concatenate([mix[s], pad], axis=1)
    wt_v[pl.ds(n_grp, 1), :] = jnp.concatenate([diag, pad], axis=1)
    wt_copy = pltpu.make_async_copy(wt_v, wt_s, wt_sem)
    wt_copy.start()
    wt_copy.wait()

    @pl.loop(0, pairs)
    def _(p):
        for s in range(n_grp + 1):
            wt_last[p, pl.ds(s, 1), :] = jnp.full((1, LANES), wt_s[s, p], F32)

    v_last[...] = vsum[chunks[-1][0]:, :]
    met_copy.wait()
    side = 2 * LANES

    @pl.loop(0, met.shape[0] // side)
    def _(t):
        q0 = pl.multiple_of(t * side, side)
        for r in range(0, met.shape[1], side):
            met_t[r:r + side, pl.ds(q0, side)] = jnp.transpose(met[pl.ds(q0, side), r:r + side])

    def wait_blocks(c):
        c0, c1 = chunks[c]
        ref = pk.at[pl.ds(0, n_dev - 1), pl.ds(c0, c1 - c0), :]
        own_copy(c).wait()
        pltpu.make_async_copy(ref, ref, a_recv.at[c]).wait()

    def fit(c):
        c0, c1 = chunks[c]
        w = c1 - c0
        left = it[:, c0:c1, :].reshape(n_grp * w, n_aux * rows)
        for q0 in range(0, n_aux * rows, side):
            f = jnp.dot(left, met_t[:, q0:q0 + side], preferred_element_type=F32)
            ft[:, pl.ds(c0, w), pl.ds(q0, side)] = f.astype(BF16).reshape(n_grp, w, side)

    def gram(c):
        c0, c1 = chunks[c]
        w = c1 - c0
        left = ft[:, c0:c1, :].reshape(n_grp * w, n_aux * rows)

        for o in range(n_grp):
            k = lax.dot_general(left, ft[o, 0:c1, :], NT, preferred_element_type=F32)
            for s in range(n_grp):
                gs[c][s * n_grp + o, :, 0:c1] = k[s * w:(s + 1) * w]

    def slots(p):
        return pair_s[0, p] // group_orbs, pair_s[1, p] // group_orbs

    def strip(c, p, part, incoming):
        c0, c1 = chunks[c]
        width = c0 if part else c1
        i, j = slots(p)
        which = j * n_grp + i if part else i * n_grp + j
        kmat = gs[c][which, :, 0:width]
        denom = vsum[c0:c1, 0:width] - wt_s[n_grp, p]
        if incoming is None:
            return -(kmat / denom)
        term = wt_s[0, p] * incoming[0, part, :, 0:width].astype(F32)
        for s in range(1, n_grp):
            term = term + wt_s[s, p] * incoming[s, part, :, 0:width].astype(F32)
        return (term - kmat) / denom

    def x_copy(c, r, d):
        return pltpu.make_async_remote_copy(
            src_ref=tx[c].at[r, d], dst_ref=rx[c].at[r, g],
            send_sem=x_send.at[r, c], recv_sem=x_recv.at[r, c],
            device_id=(a, lax.rem(g + d, n_grp)), device_id_type=MESH,
        )

    def exchange(c, r):
        c0, c1 = chunks[c]
        incoming = None if r == 0 else rx[c].at[r - 1]
        for d in list(range(1, n_grp)) + [0]:
            p = send_pair[0, lax.rem(g + d, n_grp)]
            for part in range(2 if c0 else 1):
                width = c0 if part else c1
                v = strip(c, p, part, incoming).astype(BF16)
                if d:
                    tx[c][r, d, part, :, 0:width] = v
                else:
                    rx[c][r, g, part, :, 0:width] = v
            if d:
                x_copy(c, r, d).start()

    def wait_exchange(c, r):
        ref = tx[c].at[r, pl.ds(1, n_grp - 1)]
        pltpu.make_async_copy(ref, ref, x_recv.at[r, c]).wait()

    def finish(c):
        c0, c1 = chunks[c]
        incoming = rx[c].at[ITERS - 1]

        @pl.loop(0, pairs, unroll=4)
        def _(p):
            out[p, c0:c1, 0:c1] = strip(c, p, 0, incoming)
            if c0:
                base = c0 // LANES * LANES
                top = max(c1, base + LANES)
                v = strip(c, p, 1, incoming)
                if c0 > base:
                    v = jnp.concatenate([jnp.zeros((c0 - base, c0), F32), v], axis=0)
                if c1 < top:
                    v = jnp.concatenate([v, jnp.zeros((top - c1, c0), F32)], axis=0)
                out[p, 0:c0, c0:c1] = jnp.transpose(v)[:, c0 - base:c1 - base]

    n = len(chunks)
    last = n - 1
    for t in range(n + ITERS):
        if t < n:
            wait_blocks(t)
            fit(t)
            gram(t)
            exchange(t, 0)
        for r in range(1, ITERS):
            if 0 <= t - r < n:
                wait_exchange(t - r, r - 1)
                exchange(t - r, r)
        if t + 2 < n:
            send_chunk(t + 2)
        if 0 <= t - ITERS < last:
            wait_exchange(t - ITERS, ITERS - 1)
            finish(t - ITERS)

    @pl.loop(0, pairs, unroll=4)
    def _(p):
        i, j = slots(p)
        k_last[p, 0] = gs[last][i * n_grp + j]
        k_last[p, 1] = gs[last][j * n_grp + i]

    wait_exchange(last, ITERS - 1)
    x_last[...] = rx[last][ITERS - 1]

    ref = idx_rx.at[pl.ds(1, n_aux - 1)]
    pltpu.make_async_copy(ref, ref, idx_send).wait()
    for c, (c0, c1) in enumerate(chunks):
        ref = pk.at[pl.ds(0, n_dev - 1), pl.ds(c0, c1 - c0), :]
        pltpu.make_async_copy(ref, ref, a_send.at[c]).wait()
        for r in range(ITERS):
            ref = tx[c].at[r, pl.ds(1, n_grp - 1)]
            pltpu.make_async_copy(ref, ref, x_send.at[r, c]).wait()


def last_kernel(chunk, part, k_last, x_last, wt_last, v_last, out, stage, sems):
    c0, c1 = chunk
    pairs, nv, _ = part.shape
    n_grp = x_last.shape[0]
    base = c0 // LANES * LANES
    copies = [pltpu.make_async_copy(stage.at[p], out.at[p], sems.at[p]) for p in range(pairs)]
    for p in range(pairs):

        def wide(row, width):
            v = wt_last[p, pl.ds(row, 1), :]
            v = jnp.concatenate([v] * (up(width) // LANES), axis=1)[:, :width]
            return jnp.broadcast_to(v, (c1 - c0, width))

        def strip(side, width):
            term = wide(0, width) * x_last[0, side, :, 0:width].astype(F32)
            for s in range(1, n_grp):
                term = term + wide(s, width) * x_last[s, side, :, 0:width].astype(F32)
            return (term - k_last[p, side, :, 0:width]) / (v_last[:, 0:width] - wide(n_grp, width))

        stage[p, 0:c0, :] = part[p, 0:c0, :]
        stage[p, c0:c1, :] = strip(0, c1)
        v = strip(1, c0)
        if c0 > base:
            v = jnp.concatenate([jnp.zeros((c0 - base, c0), F32), v], axis=0)
        stage[p, 0:c0, c0:c1] = jnp.transpose(v)[:, c0 - base:c1 - base]
        copies[p].start()
    for copy in copies:
        copy.wait()


def fused(integrals, metric, fock, virt_energy, send_orb, pair_orb, send_pair, cpl_slot, cpl_orb):
    rows, group_orbs, nv = integrals.shape
    n_aux = lax.axis_size("aux")
    n_grp = lax.axis_size("grp")
    naux = n_aux * rows
    od = group_orbs // n_aux
    pairs = pair_orb.shape[0]
    chunks = chunks_of(nv)
    n = len(chunks)
    dims = (n_aux, n_grp, rows, od, nv, pairs, group_orbs, chunks)
    dma = pltpu.SemaphoreType.DMA
    hbm = pl.BlockSpec(memory_space=pltpu.HBM)
    vmem = pl.BlockSpec(memory_space=pltpu.VMEM)

    def here(x):
        return pltpu.with_memory_space_constraint(x, pltpu.HBM)

    small = [
        virt_energy[None, :], send_orb, pair_orb.T, send_pair,
        cpl_slot.T, jnp.transpose(cpl_orb, (1, 2, 0)),
    ]
    parts = [(2 if c0 else 1, c1 - c0, up(c1)) for c0, c1 in chunks]
    wide = chunks[-1][1] - chunks[-1][0]
    handed = pl.pallas_call(
        functools.partial(fused_kernel, dims),
        out_shape=[
            pltpu.VMEM((pairs, nv, nv), F32),
            pltpu.VMEM((pairs, 2, wide, up(nv)), F32),
            pltpu.VMEM((n_grp, *parts[-1]), BF16),
            pltpu.VMEM((pairs, 8, LANES), F32),
            pltpu.VMEM((wide, nv), F32),
        ],
        in_specs=[hbm] * 9,
        out_specs=[vmem] * 5,
        scratch_shapes=[
            pltpu.VMEM((n_aux, rows, od, nv), BF16),
            pltpu.VMEM((n_aux * n_grp, nv, rows), BF16),
            pltpu.VMEM((n_grp, nv, naux), BF16),
            pltpu.VMEM((n_grp, nv, naux), BF16),
            pltpu.VMEM(metric.shape, BF16),
            pltpu.VMEM(metric.shape, BF16),
            pltpu.VMEM(fock.shape, BF16),
            pltpu.VMEM((nv, nv), F32),
            pltpu.VMEM((8, LANES), jnp.int32),
            pltpu.VMEM((n_aux, 8, LANES), jnp.int32),
            pltpu.VMEM((8, LANES), F32),
            pltpu.SMEM((8, LANES), F32),
            pltpu.VMEM((1, nv), F32),
            pltpu.SMEM(send_orb.shape, jnp.int32),
            pltpu.SMEM((2, pairs), jnp.int32),
            pltpu.VMEM((2, pairs), jnp.int32),
            pltpu.SMEM(send_pair.shape, jnp.int32),
            pltpu.VMEM(small[4].shape, jnp.int32),
            pltpu.VMEM(small[5].shape, jnp.int32),
            [pltpu.VMEM((n_grp * n_grp, c1 - c0, up(c1)), F32) for c0, c1 in chunks],
            [pltpu.VMEM((ITERS, n_grp, *p), BF16) for p in parts],
            [pltpu.VMEM((ITERS, n_grp, *p), BF16) for p in parts],
            dma((n_aux,)), dma, dma, dma, dma((7,)), dma, dma, dma((n,)),
            dma((n,)), dma((n,)), dma((ITERS, n)), dma((ITERS, n)), pltpu.SemaphoreType.REGULAR,
        ],
        compiler_params=pltpu.CompilerParams(
            collective_id=0, has_side_effects=True, vmem_limit_bytes=44 * 1024 * 1024
        ),
    )(*[here(x) for x in [integrals, metric, fock] + small])
    return pl.pallas_call(
        functools.partial(last_kernel, chunks[-1]),
        out_shape=jax.ShapeDtypeStruct((pairs, nv, nv), F32),
        in_specs=[vmem] * 5,
        out_specs=hbm,
        scratch_shapes=[pltpu.VMEM((pairs, nv, nv), F32), dma((pairs,))],
        compiler_params=pltpu.CompilerParams(vmem_limit_bytes=8 * 1024 * 1024),
    )(*handed)


def fits_fused(integrals, pair_orb):
    rows, group_orbs, nv = integrals.shape
    n_aux, n_grp = lax.axis_size("aux"), lax.axis_size("grp")
    return (
        rows % LANES == 0
        and nv % (2 * LANES) == 0
        and n_aux % 2 == 0
        and group_orbs == 16 * n_aux
        and n_grp < 8
        and n_grp * n_grp <= pair_orb.shape[0] <= LANES
    )


def final_kernel(idx_i, idx_j, mixing, diag, fit_ref, ve_col, ve_row, inc_ref, out_ref):
    p = pl.program_id(0)
    kmat = lax.dot_general(
        fit_ref[idx_i[p]],
        fit_ref[idx_j[p]],
        (((0,), (0,)), ((), ())),
        preferred_element_type=jnp.float32,
    )
    term = mixing[p, 0] * inc_ref[0].astype(jnp.float32)
    for s in range(1, inc_ref.shape[0]):
        term = term + mixing[p, s] * inc_ref[s].astype(jnp.float32)
    denom = (ve_col[...] + ve_row[...]) - diag[p]
    out_ref[0] = (term - kmat) / denom


def final_call(idx_i, idx_j, mixing, diag, fitted, virt_energy, incoming):
    pairs = idx_i.shape[0]
    nv = virt_energy.shape[0]
    whole = pl.BlockSpec(memory_space=pltpu.VMEM)
    return pl.pallas_call(
        final_kernel,
        out_shape=jax.ShapeDtypeStruct((pairs, nv, nv), jnp.float32),
        grid_spec=pltpu.PrefetchScalarGridSpec(
            num_scalar_prefetch=4,
            grid=(pairs,),
            in_specs=[whole, whole, whole, whole],
            out_specs=pl.BlockSpec((1, nv, nv), lambda p, *_: (p, 0, 0)),
        ),
    )(idx_i, idx_j, mixing, diag, fitted, virt_energy[:, None], virt_energy[None, :], incoming)


def stepwise(
    integrals, metric, fock, virt_energy, send_orb, pair_orb, send_pair, cpl_slot, cpl_orb
):
    rows, group_orbs, nv = integrals.shape
    n_aux = lax.axis_size("aux")
    n_grp = lax.axis_size("grp")
    orb_dev = group_orbs // n_aux
    spread = jnp.broadcast_to(send_orb, (n_aux, n_grp))
    wanted = lax.all_to_all(spread, "aux", split_axis=0, concat_axis=0, tiled=True)
    idx = (jnp.arange(n_aux, dtype=jnp.int32)[:, None] * orb_dev + wanted).reshape(-1)
    packed = jnp.transpose(jnp.take(integrals, idx, axis=1, mode="clip"), (1, 0, 2))
    block = lax.all_to_all(packed, ("aux", "grp"), split_axis=0, concat_axis=0, tiled=True)
    block = block.reshape(n_aux, n_grp, rows, nv)
    block = jnp.transpose(block, (0, 2, 1, 3)).reshape(n_aux * rows, n_grp * nv)
    fitted = jnp.dot(metric, block, preferred_element_type=jnp.float32).astype(jnp.bfloat16)
    fitted = jnp.transpose(fitted.reshape(n_aux * rows, n_grp, nv), (1, 0, 2))

    orb_i = pair_orb[:, 0]
    orb_j = pair_orb[:, 1]
    idx_i = orb_i // group_orbs
    idx_j = orb_j // group_orbs
    diag_sum = fock[orb_i, orb_i].astype(jnp.float32) + fock[orb_j, orb_j].astype(jnp.float32)
    k_orb = cpl_orb[:, :, 0]
    l_orb = cpl_orb[:, :, 1]
    first = (l_orb == orb_j[:, None]) & (k_orb != orb_i[:, None])
    second = (k_orb == orb_i[:, None]) & (l_orb != orb_j[:, None])
    f_ik = fock[orb_i[:, None], k_orb].astype(jnp.float32)
    f_jl = fock[orb_j[:, None], l_orb].astype(jnp.float32)
    weight = jnp.where(first, f_ik, 0.0) + jnp.where(second, f_jl, 0.0)
    onehot = cpl_slot[:, :, None] == jnp.arange(n_grp, dtype=jnp.int32)[None, None, :]
    mixing = jnp.sum(jnp.where(onehot, weight[:, :, None], 0.0), axis=1)

    sent = send_pair[0]
    zeros = jnp.zeros((n_grp, nv, nv), jnp.bfloat16)
    s_i, s_j, s_mix, s_diag = idx_i[sent], idx_j[sent], mixing[sent], diag_sum[sent]
    incoming = zeros
    for step in range(ITERS):
        amps = final_call(s_i, s_j, s_mix, s_diag, fitted, virt_energy, incoming)
        incoming = lax.all_to_all(
            amps.astype(jnp.bfloat16), "grp", split_axis=0, concat_axis=0, tiled=True
        )
    return final_call(idx_i, idx_j, mixing, diag_sum, fitted, virt_energy, incoming)


def on_device(*args):
    return fused(*args) if fits_fused(args[0], args[5]) else stepwise(*args)


def solution(mesh):
    in_specs = (
        P("aux", "grp", None),
        P(),
        P(),
        P(),
        P(("aux", "grp"), None),
        P(("aux", "grp"), None),
        P(("aux", "grp"), None),
        P(("aux", "grp"), None),
        P(("aux", "grp"), None, None),
    )
    out_specs = P(("aux", "grp"), None, None)
    return jax.shard_map(
        on_device, mesh=mesh, in_specs=in_specs, out_specs=out_specs, check_vma=False
    )
```

```python
import functools

import jax
import jax.numpy as jnp
from jax import lax
from jax.experimental import pallas as pl
from jax.experimental.pallas import tpu as pltpu
from jax.sharding import PartitionSpec as P

ITERS = 2
MESH = pl.DeviceIdType.MESH
F32 = jnp.float32
BF16 = jnp.bfloat16
NT = (((1,), (1,)), ((), ()))
LANES = 128


def chunks_of(nv):
    cuts = [0, nv // 2, nv * 11 // 16, nv * 13 // 16, nv * 15 // 16, nv]
    return list(zip(cuts[:-1], cuts[1:]))


def up(n):
    return -(-n // LANES) * LANES


def fused_kernel(
    dims,
    integrals, metric, fock, ve_hbm, orb_hbm, pair_hbm, mine_hbm, slot_hbm, cpl_hbm,
    out, k_last, x_last, wt_last, v_last,
    raw, pk, it, ft, met, met_t, fk, vsum, idx_tx, idx_rx, wt_v, wt_s,
    ve_row, send_orb, pair_s, pair_v, send_pair, slot_v, cpl_v,
    gs, tx, rx,
    raw_sem, met_sem, fk_sem, wt_sem, small_sem, idx_send, idx_recv, own_sem,
    a_send, a_recv, x_send, x_recv, here_sem,
):
    n_aux, n_grp, rows, od, nv, pairs, group_orbs, chunks = dims
    a = lax.axis_index("aux")
    g = lax.axis_index("grp")
    n_dev = n_aux * n_grp
    half = n_aux // 2

    def col_of(k):
        off = half + jnp.where(k % 2 == 0, k // 2, -((k + 1) // 2))
        return lax.rem(a + off, n_aux)

    def raw_copy(k, col):
        first = pl.multiple_of(col * od, od)
        return pltpu.make_async_copy(integrals.at[:, pl.ds(first, od), :], raw.at[k], raw_sem.at[k])

    small = [
        pltpu.make_async_copy(src, dst, small_sem.at[k])
        for k, (src, dst) in enumerate([
            (orb_hbm, send_orb), (mine_hbm, send_pair), (pair_hbm, pair_s), (pair_hbm, pair_v),
            (slot_hbm, slot_v), (cpl_hbm, cpl_v), (ve_hbm, ve_row),
        ])
    ]
    for copy in small:
        copy.start()
    barrier = pltpu.get_barrier_semaphore()

    row_peers = [(lax.rem(a + k, n_aux), g) for k in range(1, n_aux)]
    grp_peers = [(a, lax.rem(g + k, n_grp)) for k in range(1, n_grp)]
    for peer in row_peers + grp_peers:
        pl.semaphore_signal(barrier, inc=1, device_id=peer, device_id_type=MESH)

    @pl.loop(0, n_aux)
    def _(k):
        raw_copy(k, col_of(k)).start()

    met_copy = pltpu.make_async_copy(metric, met, met_sem)
    fk_copy = pltpu.make_async_copy(fock, fk, fk_sem)
    met_copy.start()
    fk_copy.start()
    small[0].wait()
    for s in range(n_grp):
        idx_tx[pl.ds(s, 1), :] = jnp.full((1, LANES), send_orb[0, s], jnp.int32)
        idx_rx[a, pl.ds(s, 1), :] = jnp.full((1, LANES), send_orb[0, s], jnp.int32)

    pl.semaphore_wait(barrier, n_aux - 1 + n_grp - 1)

    def idx_copy(k):
        t = lax.rem(a + k, n_aux)
        return pltpu.make_async_remote_copy(
            src_ref=idx_tx, dst_ref=idx_rx.at[a], send_sem=idx_send, recv_sem=idx_recv.at[a],
            device_id=(t, g), device_id_type=MESH,
        )

    @pl.loop(1, n_aux)
    def _(k):
        idx_copy(k).start()

    for peer in grp_peers:
        pl.semaphore_signal(here_sem, inc=1, device_id=peer, device_id_type=MESH)

    pl.semaphore_wait(here_sem, n_grp - 1)

    def block_copy(c, col, grp):
        c0, c1 = chunks[c]
        lane0 = pl.multiple_of(a * rows, rows)
        return pltpu.make_async_remote_copy(
            src_ref=pk.at[col * n_grp + grp, pl.ds(c0, c1 - c0), :],
            dst_ref=it.at[g, pl.ds(c0, c1 - c0), pl.ds(lane0, rows)],
            send_sem=a_send.at[c], recv_sem=a_recv.at[c],
            device_id=(col, grp), device_id_type=MESH,
        )

    def own_copy(c):
        c0, c1 = chunks[c]
        lane0 = pl.multiple_of(a * rows, rows)
        return pltpu.make_async_copy(
            pk.at[a * n_grp + g, pl.ds(c0, c1 - c0), :],
            it.at[g, pl.ds(c0, c1 - c0), pl.ds(lane0, rows)],
            own_sem.at[c],
        )

    def send_far(c, k):
        col = col_of(k)
        for d in range(n_grp):
            block_copy(c, col, lax.rem(g + d, n_grp)).start()

    def send_own(c):
        for d in range(1, n_grp):
            block_copy(c, a, lax.rem(g + d, n_grp)).start()
        own_copy(c).start()

    step = 2 * LANES // od
    lane = lax.broadcasted_iota(jnp.int32, (step, 2 * LANES), 1)
    row = lax.broadcasted_iota(jnp.int32, (step, 2 * LANES), 0)

    def select(k, col):
        raw_copy(k, col).wait()
        pick = []
        for s in range(n_grp):
            v = idx_rx[col, pl.ds(s, 1), :]
            v = jnp.broadcast_to(jnp.concatenate([v, v], axis=1), (step, 2 * LANES))
            pick.append(jnp.where(lane == row * od + v, 1.0, 0.0))
        sel = jnp.concatenate(pick, axis=0).astype(BF16)
        parts = []
        for t in range(rows // step):
            x = raw[k, t * step:(t + 1) * step].reshape(step * od, nv)
            parts.append(jnp.dot(sel, x, preferred_element_type=F32))
        for s in range(n_grp):
            blk = jnp.concatenate([p[s * step:(s + 1) * step] for p in parts], axis=0)
            pk[col * n_grp + s] = jnp.transpose(blk).astype(BF16)

    @pl.loop(0, n_aux - 1)
    def _(k):
        col = col_of(k)
        pltpu.make_async_copy(idx_tx, idx_tx, idx_recv.at[col]).wait()
        select(k, col)
        send_far(0, k)

    select(n_aux - 1, a)
    send_own(0)

    def send_chunk(c):
        @pl.loop(0, n_aux - 1)
        def _(k):
            send_far(c, k)

        send_own(c)

    send_chunk(1)

    for copy in small[1:]:
        copy.wait()
    ve = ve_row[...]
    vb = jnp.broadcast_to(ve, (nv, nv))
    vsum[...] = jnp.transpose(vb) + vb

    fk_copy.wait()
    orb_i = pair_v[pl.ds(0, 1), :]
    orb_j = pair_v[pl.ds(1, 1), :]
    nocc = fk.shape[0]
    orbs = lax.broadcasted_iota(jnp.int32, (nocc, pairs), 0)
    at_i = orbs == orb_i
    at_j = orbs == orb_j
    tn = (((0,), (0,)), ((), ()))
    f_i = lax.dot_general(fk[...], jnp.where(at_i, 1.0, 0.0).astype(BF16), tn, preferred_element_type=F32)
    f_j = lax.dot_general(fk[...], jnp.where(at_j, 1.0, 0.0).astype(BF16), tn, preferred_element_type=F32)

    def entry(mask, table):
        return jnp.sum(jnp.where(mask, table, 0.0), axis=0, keepdims=True)

    pad = jnp.zeros((1, LANES - pairs), F32)
    mix = [jnp.zeros((1, pairs), F32) for _ in range(n_grp)]
    for e in range(cpl_v.shape[0]):
        k_orb = cpl_v[e, pl.ds(0, 1), :]
        l_orb = cpl_v[e, pl.ds(1, 1), :]
        f_ik = entry(orbs == k_orb, f_i)
        f_jl = entry(orbs == l_orb, f_j)
        w = jnp.where((l_orb == orb_j) & (k_orb != orb_i), f_ik, 0.0)
        w = w + jnp.where((k_orb == orb_i) & (l_orb != orb_j), f_jl, 0.0)
        slot = slot_v[pl.ds(e, 1), :]
        for s in range(n_grp):
            mix[s] = mix[s] + jnp.where(slot == s, w, 0.0)
    diag = entry(at_i, f_i) + entry(at_j, f_j)
    for s in range(n_grp):
        wt_v[pl.ds(s, 1), :] = jnp.concatenate([mix[s], pad], axis=1)
    wt_v[pl.ds(n_grp, 1), :] = jnp.concatenate([diag, pad], axis=1)
    wt_copy = pltpu.make_async_copy(wt_v, wt_s, wt_sem)
    wt_copy.start()
    wt_copy.wait()

    @pl.loop(0, pairs)
    def _(p):
        for s in range(n_grp + 1):
            wt_last[p, pl.ds(s, 1), :] = jnp.full((1, LANES), wt_s[s, p], F32)

    v_last[...] = vsum[chunks[-1][0]:, :]
    met_copy.wait()
    side = 2 * LANES

    @pl.loop(0, met.shape[0] // side)
    def _(t):
        q0 = pl.multiple_of(t * side, side)
        for r in range(0, met.shape[1], side):
            met_t[r:r + side, pl.ds(q0, side)] = jnp.transpose(met[pl.ds(q0, side), r:r + side])

    def wait_blocks(c):
        c0, c1 = chunks[c]
        ref = pk.at[pl.ds(0, n_dev - 1), pl.ds(c0, c1 - c0), :]
        own_copy(c).wait()
        pltpu.make_async_copy(ref, ref, a_recv.at[c]).wait()

    def fit(c):
        c0, c1 = chunks[c]
        w = c1 - c0
        left = it[:, c0:c1, :].reshape(n_grp * w, n_aux * rows)
        for q0 in range(0, n_aux * rows, side):
            f = jnp.dot(left, met_t[:, q0:q0 + side], preferred_element_type=F32)
            ft[:, pl.ds(c0, w), pl.ds(q0, side)] = f.astype(BF16).reshape(n_grp, w, side)

    def gram(c):
        c0, c1 = chunks[c]
        w = c1 - c0
        left = ft[:, c0:c1, :].reshape(n_grp * w, n_aux * rows)

        for o in range(n_grp):
            k = lax.dot_general(left, ft[o, 0:c1, :], NT, preferred_element_type=F32)
            for s in range(n_grp):
                gs[c][s * n_grp + o, :, 0:c1] = k[s * w:(s + 1) * w]

    def slots(p):
        return pair_s[0, p] // group_orbs, pair_s[1, p] // group_orbs

    def strip(c, p, part, incoming):
        c0, c1 = chunks[c]
        width = c0 if part else c1
        i, j = slots(p)
        which = j * n_grp + i if part else i * n_grp + j
        kmat = gs[c][which, :, 0:width]
        denom = vsum[c0:c1, 0:width] - wt_s[n_grp, p]
        if incoming is None:
            return -(kmat / denom)
        term = wt_s[0, p] * incoming[0, part, :, 0:width].astype(F32)
        for s in range(1, n_grp):
            term = term + wt_s[s, p] * incoming[s, part, :, 0:width].astype(F32)
        return (term - kmat) / denom

    def x_copy(c, r, d):
        return pltpu.make_async_remote_copy(
            src_ref=tx[c].at[r, d], dst_ref=rx[c].at[r, g],
            send_sem=x_send.at[r, c], recv_sem=x_recv.at[r, c],
            device_id=(a, lax.rem(g + d, n_grp)), device_id_type=MESH,
        )

    def exchange(c, r):
        c0, c1 = chunks[c]
        incoming = None if r == 0 else rx[c].at[r - 1]
        for d in list(range(1, n_grp)) + [0]:
            p = send_pair[0, lax.rem(g + d, n_grp)]
            for part in range(2 if c0 else 1):
                width = c0 if part else c1
                v = strip(c, p, part, incoming).astype(BF16)
                if d:
                    tx[c][r, d, part, :, 0:width] = v
                else:
                    rx[c][r, g, part, :, 0:width] = v
            if d:
                x_copy(c, r, d).start()

    def wait_exchange(c, r):
        ref = tx[c].at[r, pl.ds(1, n_grp - 1)]
        pltpu.make_async_copy(ref, ref, x_recv.at[r, c]).wait()

    def finish(c):
        c0, c1 = chunks[c]
        incoming = rx[c].at[ITERS - 1]

        @pl.loop(0, pairs, unroll=4)
        def _(p):
            out[p, c0:c1, 0:c1] = strip(c, p, 0, incoming)
            if c0:
                base = c0 // LANES * LANES
                top = max(c1, base + LANES)
                v = strip(c, p, 1, incoming)
                if c0 > base:
                    v = jnp.concatenate([jnp.zeros((c0 - base, c0), F32), v], axis=0)
                if c1 < top:
                    v = jnp.concatenate([v, jnp.zeros((top - c1, c0), F32)], axis=0)
                out[p, 0:c0, c0:c1] = jnp.transpose(v)[:, c0 - base:c1 - base]

    n = len(chunks)
    last = n - 1

    def mix(c, r):
        wait_exchange(c, r - 1)
        if r < ITERS:
            exchange(c, r)
        else:
            finish(c)

    for t in range(n):
        wait_blocks(t)
        fit(t)
        gram(t)
        exchange(t, 0)
        if t + 2 == last:
            send_chunk(last)
        if t:
            mix(t - 1, 1)
        if t + 2 < last:
            send_chunk(t + 2)
        if 2 <= t < last - 1:
            mix(t - 2, 2)
    for t in range(max(last - 3, 0), last - 1):
        mix(t, 2)
    mix(last, 1)
    mix(last - 1, 2)

    @pl.loop(0, pairs, unroll=4)
    def _(p):
        i, j = slots(p)
        k_last[p, 0] = gs[last][i * n_grp + j]
        k_last[p, 1] = gs[last][j * n_grp + i]

    wait_exchange(last, ITERS - 1)
    x_last[...] = rx[last][ITERS - 1]

    ref = idx_rx.at[pl.ds(1, n_aux - 1)]
    pltpu.make_async_copy(ref, ref, idx_send).wait()
    for c, (c0, c1) in enumerate(chunks):
        ref = pk.at[pl.ds(0, n_dev - 1), pl.ds(c0, c1 - c0), :]
        pltpu.make_async_copy(ref, ref, a_send.at[c]).wait()
        for r in range(ITERS):
            ref = tx[c].at[r, pl.ds(1, n_grp - 1)]
            pltpu.make_async_copy(ref, ref, x_send.at[r, c]).wait()


def last_kernel(chunk, part, k_last, x_last, wt_last, v_last, out, stage, sems):
    c0, c1 = chunk
    pairs, nv, _ = part.shape
    n_grp = x_last.shape[0]
    base = c0 // LANES * LANES
    copies = [pltpu.make_async_copy(stage.at[p], out.at[p], sems.at[p]) for p in range(pairs)]
    for p in range(pairs):

        def wide(row, width):
            v = wt_last[p, pl.ds(row, 1), :]
            v = jnp.concatenate([v] * (up(width) // LANES), axis=1)[:, :width]
            return jnp.broadcast_to(v, (c1 - c0, width))

        def strip(side, width):
            term = wide(0, width) * x_last[0, side, :, 0:width].astype(F32)
            for s in range(1, n_grp):
                term = term + wide(s, width) * x_last[s, side, :, 0:width].astype(F32)
            return (term - k_last[p, side, :, 0:width]) / (v_last[:, 0:width] - wide(n_grp, width))

        stage[p, 0:c0, :] = part[p, 0:c0, :]
        stage[p, c0:c1, :] = strip(0, c1)
        v = strip(1, c0)
        if c0 > base:
            v = jnp.concatenate([jnp.zeros((c0 - base, c0), F32), v], axis=0)
        stage[p, 0:c0, c0:c1] = jnp.transpose(v)[:, c0 - base:c1 - base]
        copies[p].start()
    for copy in copies:
        copy.wait()


def fused(integrals, metric, fock, virt_energy, send_orb, pair_orb, send_pair, cpl_slot, cpl_orb):
    rows, group_orbs, nv = integrals.shape
    n_aux = lax.axis_size("aux")
    n_grp = lax.axis_size("grp")
    naux = n_aux * rows
    od = group_orbs // n_aux
    pairs = pair_orb.shape[0]
    chunks = chunks_of(nv)
    n = len(chunks)
    dims = (n_aux, n_grp, rows, od, nv, pairs, group_orbs, chunks)
    dma = pltpu.SemaphoreType.DMA
    hbm = pl.BlockSpec(memory_space=pltpu.HBM)
    vmem = pl.BlockSpec(memory_space=pltpu.VMEM)

    def here(x):
        return pltpu.with_memory_space_constraint(x, pltpu.HBM)

    small = [
        virt_energy[None, :], send_orb, pair_orb.T, send_pair,
        cpl_slot.T, jnp.transpose(cpl_orb, (1, 2, 0)),
    ]
    parts = [(2 if c0 else 1, c1 - c0, up(c1)) for c0, c1 in chunks]
    wide = chunks[-1][1] - chunks[-1][0]
    handed = pl.pallas_call(
        functools.partial(fused_kernel, dims),
        out_shape=[
            pltpu.VMEM((pairs, nv, nv), F32),
            pltpu.VMEM((pairs, 2, wide, up(nv)), F32),
            pltpu.VMEM((n_grp, *parts[-1]), BF16),
            pltpu.VMEM((pairs, 8, LANES), F32),
            pltpu.VMEM((wide, nv), F32),
        ],
        in_specs=[hbm] * 9,
        out_specs=[vmem] * 5,
        scratch_shapes=[
            pltpu.VMEM((n_aux, rows, od, nv), BF16),
            pltpu.VMEM((n_aux * n_grp, nv, rows), BF16),
            pltpu.VMEM((n_grp, nv, naux), BF16),
            pltpu.VMEM((n_grp, nv, naux), BF16),
            pltpu.VMEM(metric.shape, BF16),
            pltpu.VMEM(metric.shape, BF16),
            pltpu.VMEM(fock.shape, BF16),
            pltpu.VMEM((nv, nv), F32),
            pltpu.VMEM((8, LANES), jnp.int32),
            pltpu.VMEM((n_aux, 8, LANES), jnp.int32),
            pltpu.VMEM((8, LANES), F32),
            pltpu.SMEM((8, LANES), F32),
            pltpu.VMEM((1, nv), F32),
            pltpu.SMEM(send_orb.shape, jnp.int32),
            pltpu.SMEM((2, pairs), jnp.int32),
            pltpu.VMEM((2, pairs), jnp.int32),
            pltpu.SMEM(send_pair.shape, jnp.int32),
            pltpu.VMEM(small[4].shape, jnp.int32),
            pltpu.VMEM(small[5].shape, jnp.int32),
            [pltpu.VMEM((n_grp * n_grp, c1 - c0, up(c1)), F32) for c0, c1 in chunks],
            [pltpu.VMEM((ITERS, n_grp, *p), BF16) for p in parts],
            [pltpu.VMEM((ITERS, n_grp, *p), BF16) for p in parts],
            dma((n_aux,)), dma, dma, dma, dma((7,)), dma, dma((n_aux,)), dma((n,)),
            dma((n,)), dma((n,)), dma((ITERS, n)), dma((ITERS, n)), pltpu.SemaphoreType.REGULAR,
        ],
        compiler_params=pltpu.CompilerParams(
            collective_id=0, has_side_effects=True, vmem_limit_bytes=44 * 1024 * 1024
        ),
    )(*[here(x) for x in [integrals, metric, fock] + small])
    return pl.pallas_call(
        functools.partial(last_kernel, chunks[-1]),
        out_shape=jax.ShapeDtypeStruct((pairs, nv, nv), F32),
        in_specs=[vmem] * 5,
        out_specs=hbm,
        scratch_shapes=[pltpu.VMEM((pairs, nv, nv), F32), dma((pairs,))],
        compiler_params=pltpu.CompilerParams(vmem_limit_bytes=8 * 1024 * 1024),
    )(*handed)


def fits_fused(integrals, pair_orb):
    rows, group_orbs, nv = integrals.shape
    n_aux, n_grp = lax.axis_size("aux"), lax.axis_size("grp")
    return (
        rows % LANES == 0
        and nv % (2 * LANES) == 0
        and n_aux % 2 == 0
        and group_orbs == 16 * n_aux
        and n_grp < 8
        and n_grp * n_grp <= pair_orb.shape[0] <= LANES
    )


def final_kernel(idx_i, idx_j, mixing, diag, fit_ref, ve_col, ve_row, inc_ref, out_ref):
    p = pl.program_id(0)
    kmat = lax.dot_general(
        fit_ref[idx_i[p]],
        fit_ref[idx_j[p]],
        (((0,), (0,)), ((), ())),
        preferred_element_type=jnp.float32,
    )
    term = mixing[p, 0] * inc_ref[0].astype(jnp.float32)
    for s in range(1, inc_ref.shape[0]):
        term = term + mixing[p, s] * inc_ref[s].astype(jnp.float32)
    denom = (ve_col[...] + ve_row[...]) - diag[p]
    out_ref[0] = (term - kmat) / denom


def final_call(idx_i, idx_j, mixing, diag, fitted, virt_energy, incoming):
    pairs = idx_i.shape[0]
    nv = virt_energy.shape[0]
    whole = pl.BlockSpec(memory_space=pltpu.VMEM)
    return pl.pallas_call(
        final_kernel,
        out_shape=jax.ShapeDtypeStruct((pairs, nv, nv), jnp.float32),
        grid_spec=pltpu.PrefetchScalarGridSpec(
            num_scalar_prefetch=4,
            grid=(pairs,),
            in_specs=[whole, whole, whole, whole],
            out_specs=pl.BlockSpec((1, nv, nv), lambda p, *_: (p, 0, 0)),
        ),
    )(idx_i, idx_j, mixing, diag, fitted, virt_energy[:, None], virt_energy[None, :], incoming)


def stepwise(
    integrals, metric, fock, virt_energy, send_orb, pair_orb, send_pair, cpl_slot, cpl_orb
):
    rows, group_orbs, nv = integrals.shape
    n_aux = lax.axis_size("aux")
    n_grp = lax.axis_size("grp")
    orb_dev = group_orbs // n_aux
    spread = jnp.broadcast_to(send_orb, (n_aux, n_grp))
    wanted = lax.all_to_all(spread, "aux", split_axis=0, concat_axis=0, tiled=True)
    idx = (jnp.arange(n_aux, dtype=jnp.int32)[:, None] * orb_dev + wanted).reshape(-1)
    packed = jnp.transpose(jnp.take(integrals, idx, axis=1, mode="clip"), (1, 0, 2))
    block = lax.all_to_all(packed, ("aux", "grp"), split_axis=0, concat_axis=0, tiled=True)
    block = block.reshape(n_aux, n_grp, rows, nv)
    block = jnp.transpose(block, (0, 2, 1, 3)).reshape(n_aux * rows, n_grp * nv)
    fitted = jnp.dot(metric, block, preferred_element_type=jnp.float32).astype(jnp.bfloat16)
    fitted = jnp.transpose(fitted.reshape(n_aux * rows, n_grp, nv), (1, 0, 2))

    orb_i = pair_orb[:, 0]
    orb_j = pair_orb[:, 1]
    idx_i = orb_i // group_orbs
    idx_j = orb_j // group_orbs
    diag_sum = fock[orb_i, orb_i].astype(jnp.float32) + fock[orb_j, orb_j].astype(jnp.float32)
    k_orb = cpl_orb[:, :, 0]
    l_orb = cpl_orb[:, :, 1]
    first = (l_orb == orb_j[:, None]) & (k_orb != orb_i[:, None])
    second = (k_orb == orb_i[:, None]) & (l_orb != orb_j[:, None])
    f_ik = fock[orb_i[:, None], k_orb].astype(jnp.float32)
    f_jl = fock[orb_j[:, None], l_orb].astype(jnp.float32)
    weight = jnp.where(first, f_ik, 0.0) + jnp.where(second, f_jl, 0.0)
    onehot = cpl_slot[:, :, None] == jnp.arange(n_grp, dtype=jnp.int32)[None, None, :]
    mixing = jnp.sum(jnp.where(onehot, weight[:, :, None], 0.0), axis=1)

    sent = send_pair[0]
    zeros = jnp.zeros((n_grp, nv, nv), jnp.bfloat16)
    s_i, s_j, s_mix, s_diag = idx_i[sent], idx_j[sent], mixing[sent], diag_sum[sent]
    incoming = zeros
    for step in range(ITERS):
        amps = final_call(s_i, s_j, s_mix, s_diag, fitted, virt_energy, incoming)
        incoming = lax.all_to_all(
            amps.astype(jnp.bfloat16), "grp", split_axis=0, concat_axis=0, tiled=True
        )
    return final_call(idx_i, idx_j, mixing, diag_sum, fitted, virt_energy, incoming)


def on_device(*args):
    return fused(*args) if fits_fused(args[0], args[5]) else stepwise(*args)


def solution(mesh):
    in_specs = (
        P("aux", "grp", None),
        P(),
        P(),
        P(),
        P(("aux", "grp"), None),
        P(("aux", "grp"), None),
        P(("aux", "grp"), None),
        P(("aux", "grp"), None),
        P(("aux", "grp"), None, None),
    )
    out_specs = P(("aux", "grp"), None, None)
    return jax.shard_map(
        on_device, mesh=mesh, in_specs=in_specs, out_specs=out_specs, check_vma=False
    )
```

```python
import functools

import jax
import jax.numpy as jnp
from jax import lax
from jax.experimental import pallas as pl
from jax.experimental.pallas import tpu as pltpu
from jax.sharding import PartitionSpec as P

ITERS = 2
MESH = pl.DeviceIdType.MESH
F32 = jnp.float32
BF16 = jnp.bfloat16
NT = (((1,), (1,)), ((), ()))
LANES = 128


def chunks_of(nv):
    cuts = [0, nv // 2, nv * 11 // 16, nv * 13 // 16, nv * 15 // 16, nv]
    return list(zip(cuts[:-1], cuts[1:]))


def up(n):
    return -(-n // LANES) * LANES


def fused_kernel(
    dims,
    integrals, metric, fock, ve_hbm, orb_hbm, pair_hbm, mine_hbm, slot_hbm, cpl_hbm,
    out, k_last, x_last, wt_last, v_last,
    raw, pk, it, ft, met, met_t, fk, vsum, idx_tx, idx_rx, wt_v, wt_s,
    ve_row, send_orb, pair_s, pair_v, send_pair, slot_v, cpl_v,
    gs, tx, rx,
    raw_sem, met_sem, fk_sem, wt_sem, small_sem, idx_send, idx_recv, own_sem,
    a_send, a_recv, x_send, x_recv, here_sem,
):
    n_aux, n_grp, rows, od, nv, pairs, group_orbs, chunks = dims
    a = lax.axis_index("aux")
    g = lax.axis_index("grp")
    n_dev = n_aux * n_grp
    half = n_aux // 2

    def col_of(k):
        off = half + jnp.where(k % 2 == 0, k // 2, -((k + 1) // 2))
        return lax.rem(a + off, n_aux)

    def raw_copy(k, col):
        first = pl.multiple_of(col * od, od)
        return pltpu.make_async_copy(integrals.at[:, pl.ds(first, od), :], raw.at[k], raw_sem.at[k])

    small = [
        pltpu.make_async_copy(src, dst, small_sem.at[k])
        for k, (src, dst) in enumerate([
            (orb_hbm, send_orb), (mine_hbm, send_pair), (pair_hbm, pair_s), (pair_hbm, pair_v),
            (slot_hbm, slot_v), (cpl_hbm, cpl_v), (ve_hbm, ve_row),
        ])
    ]
    for copy in small:
        copy.start()
    barrier = pltpu.get_barrier_semaphore()

    row_peers = [(lax.rem(a + k, n_aux), g) for k in range(1, n_aux)]
    grp_peers = [(a, lax.rem(g + k, n_grp)) for k in range(1, n_grp)]
    for peer in row_peers + grp_peers:
        pl.semaphore_signal(barrier, inc=1, device_id=peer, device_id_type=MESH)

    @pl.loop(0, n_aux)
    def _(k):
        raw_copy(k, col_of(k)).start()

    met_copy = pltpu.make_async_copy(metric, met, met_sem)
    fk_copy = pltpu.make_async_copy(fock, fk, fk_sem)
    met_copy.start()
    fk_copy.start()
    small[0].wait()
    for s in range(n_grp):
        idx_tx[pl.ds(s, 1), :] = jnp.full((1, LANES), send_orb[0, s], jnp.int32)
        idx_rx[a, pl.ds(s, 1), :] = jnp.full((1, LANES), send_orb[0, s], jnp.int32)

    pl.semaphore_wait(barrier, n_aux - 1 + n_grp - 1)

    def idx_copy(k):
        t = lax.rem(a + k, n_aux)
        return pltpu.make_async_remote_copy(
            src_ref=idx_tx, dst_ref=idx_rx.at[a], send_sem=idx_send, recv_sem=idx_recv.at[a],
            device_id=(t, g), device_id_type=MESH,
        )

    @pl.loop(1, n_aux)
    def _(k):
        idx_copy(k).start()

    for peer in grp_peers:
        pl.semaphore_signal(here_sem, inc=1, device_id=peer, device_id_type=MESH)

    pl.semaphore_wait(here_sem, n_grp - 1)

    def block_copy(c, col, grp):
        c0, c1 = chunks[c]
        lane0 = pl.multiple_of(a * rows, rows)
        return pltpu.make_async_remote_copy(
            src_ref=pk.at[col * n_grp + grp, pl.ds(c0, c1 - c0), :],
            dst_ref=it.at[g, pl.ds(c0, c1 - c0), pl.ds(lane0, rows)],
            send_sem=a_send.at[c], recv_sem=a_recv.at[c],
            device_id=(col, grp), device_id_type=MESH,
        )

    def own_copy(c):
        c0, c1 = chunks[c]
        lane0 = pl.multiple_of(a * rows, rows)
        return pltpu.make_async_copy(
            pk.at[a * n_grp + g, pl.ds(c0, c1 - c0), :],
            it.at[g, pl.ds(c0, c1 - c0), pl.ds(lane0, rows)],
            own_sem.at[c],
        )

    def send_far(c, k):
        col = col_of(k)
        for d in range(n_grp):
            block_copy(c, col, lax.rem(g + d, n_grp)).start()

    def send_own(c):
        for d in range(1, n_grp):
            block_copy(c, a, lax.rem(g + d, n_grp)).start()
        own_copy(c).start()

    step = 2 * LANES // od
    lane = lax.broadcasted_iota(jnp.int32, (step, 2 * LANES), 1)
    row = lax.broadcasted_iota(jnp.int32, (step, 2 * LANES), 0)

    def select(k, col):
        raw_copy(k, col).wait()
        pick = []
        for s in range(n_grp):
            v = idx_rx[col, pl.ds(s, 1), :]
            v = jnp.broadcast_to(jnp.concatenate([v, v], axis=1), (step, 2 * LANES))
            pick.append(jnp.where(lane == row * od + v, 1.0, 0.0))
        sel = jnp.concatenate(pick, axis=0).astype(BF16)
        parts = []
        for t in range(rows // step):
            x = raw[k, t * step:(t + 1) * step].reshape(step * od, nv)
            parts.append(jnp.dot(sel, x, preferred_element_type=F32))
        for s in range(n_grp):
            blk = jnp.concatenate([p[s * step:(s + 1) * step] for p in parts], axis=0)
            pk[col * n_grp + s] = jnp.transpose(blk).astype(BF16)

    @pl.loop(0, n_aux - 1)
    def _(k):
        col = col_of(k)
        pltpu.make_async_copy(idx_tx, idx_tx, idx_recv.at[col]).wait()
        select(k, col)
        send_far(0, k)

    select(n_aux - 1, a)
    send_own(0)

    def send_chunk(c):
        @pl.loop(0, n_aux - 1)
        def _(k):
            send_far(c, k)

        send_own(c)

    send_chunk(1)

    for copy in small[1:]:
        copy.wait()
    ve = ve_row[...]
    vb = jnp.broadcast_to(ve, (nv, nv))
    vsum[...] = jnp.transpose(vb) + vb

    fk_copy.wait()
    orb_i = pair_v[pl.ds(0, 1), :]
    orb_j = pair_v[pl.ds(1, 1), :]
    nocc = fk.shape[0]
    orbs = lax.broadcasted_iota(jnp.int32, (nocc, pairs), 0)
    at_i = orbs == orb_i
    at_j = orbs == orb_j
    tn = (((0,), (0,)), ((), ()))
    f_i = lax.dot_general(fk[...], jnp.where(at_i, 1.0, 0.0).astype(BF16), tn, preferred_element_type=F32)
    f_j = lax.dot_general(fk[...], jnp.where(at_j, 1.0, 0.0).astype(BF16), tn, preferred_element_type=F32)

    def entry(mask, table):
        return jnp.sum(jnp.where(mask, table, 0.0), axis=0, keepdims=True)

    pad = jnp.zeros((1, LANES - pairs), F32)
    mix = [jnp.zeros((1, pairs), F32) for _ in range(n_grp)]
    for e in range(cpl_v.shape[0]):
        k_orb = cpl_v[e, pl.ds(0, 1), :]
        l_orb = cpl_v[e, pl.ds(1, 1), :]
        f_ik = entry(orbs == k_orb, f_i)
        f_jl = entry(orbs == l_orb, f_j)
        w = jnp.where((l_orb == orb_j) & (k_orb != orb_i), f_ik, 0.0)
        w = w + jnp.where((k_orb == orb_i) & (l_orb != orb_j), f_jl, 0.0)
        slot = slot_v[pl.ds(e, 1), :]
        for s in range(n_grp):
            mix[s] = mix[s] + jnp.where(slot == s, w, 0.0)
    diag = entry(at_i, f_i) + entry(at_j, f_j)
    for s in range(n_grp):
        wt_v[pl.ds(s, 1), :] = jnp.concatenate([mix[s], pad], axis=1)
    wt_v[pl.ds(n_grp, 1), :] = jnp.concatenate([diag, pad], axis=1)
    wt_copy = pltpu.make_async_copy(wt_v, wt_s, wt_sem)
    wt_copy.start()
    wt_copy.wait()

    @pl.loop(0, pairs)
    def _(p):
        for s in range(n_grp + 1):
            wt_last[p, pl.ds(s, 1), :] = jnp.full((1, LANES), wt_s[s, p], F32)

    v_last[...] = vsum[chunks[-1][0]:, :]
    met_copy.wait()
    side = 2 * LANES

    @pl.loop(0, met.shape[0] // side)
    def _(t):
        q0 = pl.multiple_of(t * side, side)
        for r in range(0, met.shape[1], side):
            met_t[r:r + side, pl.ds(q0, side)] = jnp.transpose(met[pl.ds(q0, side), r:r + side])

    def wait_blocks(c):
        c0, c1 = chunks[c]
        ref = pk.at[pl.ds(0, n_dev - 1), pl.ds(c0, c1 - c0), :]
        own_copy(c).wait()
        pltpu.make_async_copy(ref, ref, a_recv.at[c]).wait()

    def fit(c):
        c0, c1 = chunks[c]
        w = c1 - c0
        left = it[:, c0:c1, :].reshape(n_grp * w, n_aux * rows)
        for q0 in range(0, n_aux * rows, side):
            f = jnp.dot(left, met_t[:, q0:q0 + side], preferred_element_type=F32)
            ft[:, pl.ds(c0, w), pl.ds(q0, side)] = f.astype(BF16).reshape(n_grp, w, side)

    def gram(c):
        c0, c1 = chunks[c]
        w = c1 - c0
        left = ft[:, c0:c1, :].reshape(n_grp * w, n_aux * rows)

        for o in range(n_grp):
            k = lax.dot_general(left, ft[o, 0:c1, :], NT, preferred_element_type=F32)
            for s in range(n_grp):
                gs[c][s * n_grp + o, :, 0:c1] = k[s * w:(s + 1) * w]

    def slots(p):
        return pair_s[0, p] // group_orbs, pair_s[1, p] // group_orbs

    def strip(c, p, part, incoming):
        c0, c1 = chunks[c]
        width = c0 if part else c1
        i, j = slots(p)
        which = j * n_grp + i if part else i * n_grp + j
        kmat = gs[c][which, :, 0:width]
        denom = vsum[c0:c1, 0:width] - wt_s[n_grp, p]
        if incoming is None:
            return -(kmat / denom)
        off = up(c1) if part else 0
        term = wt_s[0, p] * incoming[0, :, off:off + width].astype(F32)
        for s in range(1, n_grp):
            term = term + wt_s[s, p] * incoming[s, :, off:off + width].astype(F32)
        return (term - kmat) / denom

    def x_copy(c, r, d):
        return pltpu.make_async_remote_copy(
            src_ref=tx[c].at[r, d], dst_ref=rx[c].at[r, g],
            send_sem=x_send.at[r, c], recv_sem=x_recv.at[r, c],
            device_id=(a, lax.rem(g + d, n_grp)), device_id_type=MESH,
        )

    def exchange(c, r):
        c0, c1 = chunks[c]
        incoming = None if r == 0 else rx[c].at[r - 1]
        for d in list(range(1, n_grp)) + [0]:
            p = send_pair[0, lax.rem(g + d, n_grp)]
            for part in range(2 if c0 else 1):
                width = c0 if part else c1
                off = up(c1) if part else 0
                v = strip(c, p, part, incoming).astype(BF16)
                if d:
                    tx[c][r, d, :, off:off + width] = v
                else:
                    rx[c][r, g, :, off:off + width] = v
            if d:
                x_copy(c, r, d).start()

    def wait_exchange(c, r):
        ref = tx[c].at[r, pl.ds(1, n_grp - 1)]
        pltpu.make_async_copy(ref, ref, x_recv.at[r, c]).wait()

    def finish(c):
        c0, c1 = chunks[c]
        incoming = rx[c].at[ITERS - 1]

        @pl.loop(0, pairs, unroll=4)
        def _(p):
            out[p, c0:c1, 0:c1] = strip(c, p, 0, incoming)
            if c0:
                base = c0 // LANES * LANES
                top = max(c1, base + LANES)
                v = strip(c, p, 1, incoming)
                if c0 > base:
                    v = jnp.concatenate([jnp.zeros((c0 - base, c0), F32), v], axis=0)
                if c1 < top:
                    v = jnp.concatenate([v, jnp.zeros((top - c1, c0), F32)], axis=0)
                out[p, 0:c0, c0:c1] = jnp.transpose(v)[:, c0 - base:c1 - base]

    n = len(chunks)
    last = n - 1

    def mix(c, r):
        wait_exchange(c, r - 1)
        if r < ITERS:
            exchange(c, r)
        else:
            finish(c)

    for t in range(n):
        wait_blocks(t)
        fit(t)
        gram(t)
        exchange(t, 0)
        if t + 2 == last:
            send_chunk(last)
        if t:
            mix(t - 1, 1)
        if t + 2 < last:
            send_chunk(t + 2)
        if 2 <= t < last - 1:
            mix(t - 2, 2)
    for t in range(max(last - 3, 0), last - 1):
        mix(t, 2)
    mix(last, 1)
    mix(last - 1, 2)

    @pl.loop(0, pairs, unroll=4)
    def _(p):
        i, j = slots(p)
        k_last[p, 0] = gs[last][i * n_grp + j]
        k_last[p, 1] = gs[last][j * n_grp + i]

    wait_exchange(last, ITERS - 1)
    x_last[...] = rx[last][ITERS - 1]

    ref = idx_rx.at[pl.ds(1, n_aux - 1)]
    pltpu.make_async_copy(ref, ref, idx_send).wait()
    for c, (c0, c1) in enumerate(chunks):
        ref = pk.at[pl.ds(0, n_dev - 1), pl.ds(c0, c1 - c0), :]
        pltpu.make_async_copy(ref, ref, a_send.at[c]).wait()
        for r in range(ITERS):
            ref = tx[c].at[r, pl.ds(1, n_grp - 1)]
            pltpu.make_async_copy(ref, ref, x_send.at[r, c]).wait()


def last_kernel(chunk, part, k_last, x_last, wt_last, v_last, out, stage, sems):
    c0, c1 = chunk
    pairs, nv, _ = part.shape
    n_grp = x_last.shape[0]
    base = c0 // LANES * LANES
    copies = [pltpu.make_async_copy(stage.at[p], out.at[p], sems.at[p]) for p in range(pairs)]
    for p in range(pairs):

        def wide(row, width):
            v = wt_last[p, pl.ds(row, 1), :]
            v = jnp.concatenate([v] * (up(width) // LANES), axis=1)[:, :width]
            return jnp.broadcast_to(v, (c1 - c0, width))

        def strip(side, width):
            off = up(c1) if side else 0
            term = wide(0, width) * x_last[0, :, off:off + width].astype(F32)
            for s in range(1, n_grp):
                term = term + wide(s, width) * x_last[s, :, off:off + width].astype(F32)
            return (term - k_last[p, side, :, 0:width]) / (v_last[:, 0:width] - wide(n_grp, width))

        stage[p, 0:c0, :] = part[p, 0:c0, :]
        stage[p, c0:c1, :] = strip(0, c1)
        v = strip(1, c0)
        if c0 > base:
            v = jnp.concatenate([jnp.zeros((c0 - base, c0), F32), v], axis=0)
        stage[p, 0:c0, c0:c1] = jnp.transpose(v)[:, c0 - base:c1 - base]
        copies[p].start()
    for copy in copies:
        copy.wait()


def fused(integrals, metric, fock, virt_energy, send_orb, pair_orb, send_pair, cpl_slot, cpl_orb):
    rows, group_orbs, nv = integrals.shape
    n_aux = lax.axis_size("aux")
    n_grp = lax.axis_size("grp")
    naux = n_aux * rows
    od = group_orbs // n_aux
    pairs = pair_orb.shape[0]
    chunks = chunks_of(nv)
    n = len(chunks)
    dims = (n_aux, n_grp, rows, od, nv, pairs, group_orbs, chunks)
    dma = pltpu.SemaphoreType.DMA
    hbm = pl.BlockSpec(memory_space=pltpu.HBM)
    vmem = pl.BlockSpec(memory_space=pltpu.VMEM)

    def here(x):
        return pltpu.with_memory_space_constraint(x, pltpu.HBM)

    small = [
        virt_energy[None, :], send_orb, pair_orb.T, send_pair,
        cpl_slot.T, jnp.transpose(cpl_orb, (1, 2, 0)),
    ]
    parts = [(c1 - c0, up(c1) + up(c0)) for c0, c1 in chunks]
    wide = chunks[-1][1] - chunks[-1][0]
    handed = pl.pallas_call(
        functools.partial(fused_kernel, dims),
        out_shape=[
            pltpu.VMEM((pairs, nv, nv), F32),
            pltpu.VMEM((pairs, 2, wide, up(nv)), F32),
            pltpu.VMEM((n_grp, *parts[-1]), BF16),
            pltpu.VMEM((pairs, 8, LANES), F32),
            pltpu.VMEM((wide, nv), F32),
        ],
        in_specs=[hbm] * 9,
        out_specs=[vmem] * 5,
        scratch_shapes=[
            pltpu.VMEM((n_aux, rows, od, nv), BF16),
            pltpu.VMEM((n_aux * n_grp, nv, rows), BF16),
            pltpu.VMEM((n_grp, nv, naux), BF16),
            pltpu.VMEM((n_grp, nv, naux), BF16),
            pltpu.VMEM(metric.shape, BF16),
            pltpu.VMEM(metric.shape, BF16),
            pltpu.VMEM(fock.shape, BF16),
            pltpu.VMEM((nv, nv), F32),
            pltpu.VMEM((8, LANES), jnp.int32),
            pltpu.VMEM((n_aux, 8, LANES), jnp.int32),
            pltpu.VMEM((8, LANES), F32),
            pltpu.SMEM((8, LANES), F32),
            pltpu.VMEM((1, nv), F32),
            pltpu.SMEM(send_orb.shape, jnp.int32),
            pltpu.SMEM((2, pairs), jnp.int32),
            pltpu.VMEM((2, pairs), jnp.int32),
            pltpu.SMEM(send_pair.shape, jnp.int32),
            pltpu.VMEM(small[4].shape, jnp.int32),
            pltpu.VMEM(small[5].shape, jnp.int32),
            [pltpu.VMEM((n_grp * n_grp, c1 - c0, up(c1)), F32) for c0, c1 in chunks],
            [pltpu.VMEM((ITERS, n_grp, *p), BF16) for p in parts],
            [pltpu.VMEM((ITERS, n_grp, *p), BF16) for p in parts],
            dma((n_aux,)), dma, dma, dma, dma((7,)), dma, dma((n_aux,)), dma((n,)),
            dma((n,)), dma((n,)), dma((ITERS, n)), dma((ITERS, n)), pltpu.SemaphoreType.REGULAR,
        ],
        compiler_params=pltpu.CompilerParams(
            collective_id=0, has_side_effects=True, vmem_limit_bytes=44 * 1024 * 1024
        ),
    )(*[here(x) for x in [integrals, metric, fock] + small])
    return pl.pallas_call(
        functools.partial(last_kernel, chunks[-1]),
        out_shape=jax.ShapeDtypeStruct((pairs, nv, nv), F32),
        in_specs=[vmem] * 5,
        out_specs=hbm,
        scratch_shapes=[pltpu.VMEM((pairs, nv, nv), F32), dma((pairs,))],
        compiler_params=pltpu.CompilerParams(vmem_limit_bytes=8 * 1024 * 1024),
    )(*handed)


def fits_fused(integrals, pair_orb):
    rows, group_orbs, nv = integrals.shape
    n_aux, n_grp = lax.axis_size("aux"), lax.axis_size("grp")
    return (
        rows % LANES == 0
        and nv % (2 * LANES) == 0
        and n_aux % 2 == 0
        and group_orbs == 16 * n_aux
        and n_grp < 8
        and n_grp * n_grp <= pair_orb.shape[0] <= LANES
    )


def final_kernel(idx_i, idx_j, mixing, diag, fit_ref, ve_col, ve_row, inc_ref, out_ref):
    p = pl.program_id(0)
    kmat = lax.dot_general(
        fit_ref[idx_i[p]],
        fit_ref[idx_j[p]],
        (((0,), (0,)), ((), ())),
        preferred_element_type=jnp.float32,
    )
    term = mixing[p, 0] * inc_ref[0].astype(jnp.float32)
    for s in range(1, inc_ref.shape[0]):
        term = term + mixing[p, s] * inc_ref[s].astype(jnp.float32)
    denom = (ve_col[...] + ve_row[...]) - diag[p]
    out_ref[0] = (term - kmat) / denom


def final_call(idx_i, idx_j, mixing, diag, fitted, virt_energy, incoming):
    pairs = idx_i.shape[0]
    nv = virt_energy.shape[0]
    whole = pl.BlockSpec(memory_space=pltpu.VMEM)
    return pl.pallas_call(
        final_kernel,
        out_shape=jax.ShapeDtypeStruct((pairs, nv, nv), jnp.float32),
        grid_spec=pltpu.PrefetchScalarGridSpec(
            num_scalar_prefetch=4,
            grid=(pairs,),
            in_specs=[whole, whole, whole, whole],
            out_specs=pl.BlockSpec((1, nv, nv), lambda p, *_: (p, 0, 0)),
        ),
    )(idx_i, idx_j, mixing, diag, fitted, virt_energy[:, None], virt_energy[None, :], incoming)


def stepwise(
    integrals, metric, fock, virt_energy, send_orb, pair_orb, send_pair, cpl_slot, cpl_orb
):
    rows, group_orbs, nv = integrals.shape
    n_aux = lax.axis_size("aux")
    n_grp = lax.axis_size("grp")
    orb_dev = group_orbs // n_aux
    spread = jnp.broadcast_to(send_orb, (n_aux, n_grp))
    wanted = lax.all_to_all(spread, "aux", split_axis=0, concat_axis=0, tiled=True)
    idx = (jnp.arange(n_aux, dtype=jnp.int32)[:, None] * orb_dev + wanted).reshape(-1)
    packed = jnp.transpose(jnp.take(integrals, idx, axis=1, mode="clip"), (1, 0, 2))
    block = lax.all_to_all(packed, ("aux", "grp"), split_axis=0, concat_axis=0, tiled=True)
    block = block.reshape(n_aux, n_grp, rows, nv)
    block = jnp.transpose(block, (0, 2, 1, 3)).reshape(n_aux * rows, n_grp * nv)
    fitted = jnp.dot(metric, block, preferred_element_type=jnp.float32).astype(jnp.bfloat16)
    fitted = jnp.transpose(fitted.reshape(n_aux * rows, n_grp, nv), (1, 0, 2))

    orb_i = pair_orb[:, 0]
    orb_j = pair_orb[:, 1]
    idx_i = orb_i // group_orbs
    idx_j = orb_j // group_orbs
    diag_sum = fock[orb_i, orb_i].astype(jnp.float32) + fock[orb_j, orb_j].astype(jnp.float32)
    k_orb = cpl_orb[:, :, 0]
    l_orb = cpl_orb[:, :, 1]
    first = (l_orb == orb_j[:, None]) & (k_orb != orb_i[:, None])
    second = (k_orb == orb_i[:, None]) & (l_orb != orb_j[:, None])
    f_ik = fock[orb_i[:, None], k_orb].astype(jnp.float32)
    f_jl = fock[orb_j[:, None], l_orb].astype(jnp.float32)
    weight = jnp.where(first, f_ik, 0.0) + jnp.where(second, f_jl, 0.0)
    onehot = cpl_slot[:, :, None] == jnp.arange(n_grp, dtype=jnp.int32)[None, None, :]
    mixing = jnp.sum(jnp.where(onehot, weight[:, :, None], 0.0), axis=1)

    sent = send_pair[0]
    zeros = jnp.zeros((n_grp, nv, nv), jnp.bfloat16)
    s_i, s_j, s_mix, s_diag = idx_i[sent], idx_j[sent], mixing[sent], diag_sum[sent]
    incoming = zeros
    for step in range(ITERS):
        amps = final_call(s_i, s_j, s_mix, s_diag, fitted, virt_energy, incoming)
        incoming = lax.all_to_all(
            amps.astype(jnp.bfloat16), "grp", split_axis=0, concat_axis=0, tiled=True
        )
    return final_call(idx_i, idx_j, mixing, diag_sum, fitted, virt_energy, incoming)


def on_device(*args):
    return fused(*args) if fits_fused(args[0], args[5]) else stepwise(*args)


def solution(mesh):
    in_specs = (
        P("aux", "grp", None),
        P(),
        P(),
        P(),
        P(("aux", "grp"), None),
        P(("aux", "grp"), None),
        P(("aux", "grp"), None),
        P(("aux", "grp"), None),
        P(("aux", "grp"), None, None),
    )
    out_specs = P(("aux", "grp"), None, None)
    return jax.shard_map(
        on_device, mesh=mesh, in_specs=in_specs, out_specs=out_specs, check_vma=False
    )
```
